128 devices in a mesh: gx: 8 (over z_hi, y), gy: 16 (over z_lo, x, core).
Axes of the slice: x: 4, y: 4, z: 4 (z_hi: 2, z_lo: 2; z = z_hi * 2 + z_lo), core: 2. Of those that a mesh axis runs over, the one named last changes fastest.
Arguments:
- adjoint_e: bfloat16 [3, 256, 1024, 128], P(None, 'gx', 'gy'), may hold values from -6 to 6
- adjoint_h: bfloat16 [3, 256, 1024, 128], P(None, 'gx', 'gy'), may hold values from -6 to 6
- material: int32 [256, 1024, 128], P('gx', 'gy'), may hold values from 0 to 3
- inv_eps: float32 [4], replicated, may hold values from 0.08 to 1
- forward_design: bfloat16 [3, 256, 1024, 128], P(None, 'gx', 'gy'), may hold values from -6 to 6
- cell_slot: int32 [256, 1024], P('gx', 'gy'), may hold values from 0 to 511, as said below
- tile_pillars: int32 [8, 16, 512], replicated, may hold values from -1 to 65535, as said below
- pillar_rank: int32 [65536], replicated, may hold values from 0 to 65535, as said below
Outputs:
- new_e: bfloat16 [3, 256, 1024, 128], P(None, 'gx', 'gy')
- new_h: bfloat16 [3, 256, 1024, 128], P(None, 'gx', 'gy')
- gradient: float32 [32, 65536], P(None, ('gx', 'gy'))
The draws below stay inside these ranges and needn't reach their ends.
Inputs may be any that keep to these rules, and one draw needn't show every extreme that they name: `cell_slot`: the cell's slot holds the id of the pillar that covers the cell. `tile_pillars`: pillars are rectangles of 2 or 3 cells along x and along y that tile the lateral grid and never cross a tile's border. The lx-th pillar along x and ly-th along y of tile (tx, ty), counted from the tile's low corner, has id (tx * 16 + lx) * 512 + ty * 32 + ly. Each tile lists every pillar in it exactly once, in no particular order, with -1 in unused slots; tile (0, 0) uses all 512 slots. `pillar_rank`: A permutation of the pillar ids; rank r is owned by device r // 512 of gx+gy. Of the 512 ids of one tile, exactly 4 have ranks owned by each device.
All inputs are finite; a program needn't handle non-finite values.
Results may differ from the reference program's by a relative error of at most 0.0049.
Values may be sent and summed in bfloat16 or wider, within the bound.
No kernel may reach another device: no remote copies, remote signals or barrier semaphores. Data moves between devices by JAX's collectives and lax.ppermute only.
A program may use at most 128 MiB of HBM per device.

```python
import math
import jax
import jax.numpy as jnp
from jax import lax

CX = 32
CY = 64
NZ = 128
DZ = 128
DL = 32
NMAT = 4
NX = 256
NY = 1024
KY = 512
P_SIZE = 65536
PT = 512


def axis_pillars(key, cells, tile_cells):
    segments = cells // tile_cells
    half = tile_cells // 2
    key_wide, key_turn = jax.random.split(key)
    wide_count = 2 * jax.random.randint(key_wide, (segments,), 0, tile_cells // 6 + 1)
    wide_count = wide_count.at[0].set(0).astype(jnp.int32)
    count = (half - wide_count // 2).astype(jnp.int32)
    turn = (jax.random.randint(key_turn, (segments,), 0, half) % count).astype(jnp.int32)
    steps = jnp.arange(half, dtype=jnp.int32)[None, :]
    shifted = steps + turn[:, None]
    wide = (shifted + 1) * wide_count[:, None] // count[:, None] - shifted * wide_count[:, None] // count[:, None]
    widths = jnp.where(steps < count[:, None], 2 + wide, 0).astype(jnp.int32)
    ends = jnp.cumsum(widths, axis=1)
    local_cells = jnp.arange(tile_cells, dtype=jnp.int32)
    local = jnp.sum((ends[:, None, :] <= local_cells[None, :, None]).astype(jnp.int32), axis=2)
    return (local.reshape(cells).astype(jnp.int32), count)


def pillar_lattice(key):
    base = jax.random.fold_in(key, 7)
    key_x, key_y, key_order = jax.random.split(base, 3)
    local_x, count_x = axis_pillars(key_x, NX, CX)
    local_y, count_y = axis_pillars(key_y, NY, CY)
    half_x = CX // 2
    half_y = CY // 2
    tiles_x = NX // CX
    tiles_y = NY // CY
    canon = jnp.arange(PT, dtype=jnp.int32)
    along_x = canon // half_y
    along_y = canon % half_y
    tile_x = jnp.arange(tiles_x, dtype=jnp.int32)[:, None, None]
    tile_y = jnp.arange(tiles_y, dtype=jnp.int32)[None, :, None]
    exists = (along_x[None, None, :] < count_x[:, None, None]) & (along_y[None, None, :] < count_y[None, :, None])
    ids = (tile_x * half_x + along_x[None, None, :]) * KY + tile_y * half_y + along_y[None, None, :]
    ids = jnp.where(exists, ids, -1).astype(jnp.int32)
    keys = jax.random.split(key_order, tiles_x * tiles_y)
    orders = jax.vmap(lambda one: jax.random.permutation(one, PT))(keys).reshape(tiles_x, tiles_y, PT).astype(jnp.int32)
    listed = jnp.take_along_axis(ids, orders, axis=2).astype(jnp.int32)
    inverse = jnp.argsort(orders, axis=2).astype(jnp.int32)
    cell_tx = (jnp.arange(NX) // CX).astype(jnp.int32)
    cell_ty = (jnp.arange(NY) // CY).astype(jnp.int32)
    position = local_x[:, None] * half_y + local_y[None, :]
    cell_slot = inverse[cell_tx[:, None], cell_ty[None, :], position]
    return (cell_slot.astype(jnp.int32), listed)


def draw_cell_slot(key, part):
    return pillar_lattice(key)[0]


def draw_tile_pillars(key, part):
    return pillar_lattice(key)[1]


def draw_pillar_rank(key, part):
    tiles_y = NY // CY
    tiles = NX // CX * tiles_y
    room = PT // tiles
    half_x = CX // 2
    half_y = CY // 2
    keys = jax.random.split(jax.random.fold_in(key, 11), tiles)
    perms = jax.vmap(lambda one: jax.random.permutation(one, PT))(keys).astype(jnp.int32)
    ident = jnp.arange(P_SIZE, dtype=jnp.int32)
    index_x = ident // KY
    index_y = ident % KY
    tile = index_x // half_x * tiles_y + index_y // half_y
    canon = index_x % half_x * half_y + index_y % half_y
    picked = perms[tile, canon]
    owner = (picked + tile) % tiles
    return (owner * PT + tile * room + picked // tiles).astype(jnp.int32)


def with_ends(entries, own_key, low, largest):
    dims = entries.shape
    place = [jax.random.randint(jax.random.fold_in(own_key, axis), (), 0, dims[axis]) for axis in range(len(dims))]
    entries = entries.at[tuple(place)].set(low)
    longest = dims.index(max(dims))
    place[longest] = (place[longest] + 1) % dims[longest]
    return entries.at[tuple(place)].set(largest)


def block_levels(rng, shape, shards, low, high):
    level, own = 1.0, jax.random.fold_in(rng, 6)
    for dim, blocks in shards:
        heights = jnp.exp(jax.random.uniform(jax.random.fold_in(own, dim), (blocks,), jnp.float32, low / len(shards), high / len(shards)))
        level = level * jnp.repeat(heights, shape[dim] // blocks).reshape([-1 if axis == dim else 1 for axis in range(len(shape))])
    return level


def centred(stream_key, extent, deviation, bound, cuts=(), held_as=jnp.bfloat16):
    array = deviation * jax.random.normal(stream_key, extent, jnp.float32)
    if cuts:
        array = array * block_levels(stream_key, extent, cuts, -0.22, 0.18)
    return jnp.clip(array, -bound, bound).astype(held_as)


def setup_inputs(seed: int = 0) -> dict:
    streams_of = jax.random.split(jax.random.key(seed), 9)
    return {
        "adjoint_e": centred(streams_of[0], (3, NX, NY, NZ), 1.0, 6.0, ((1, 8), (2, 16))),
        "adjoint_h": centred(streams_of[1], (3, NX, NY, NZ), 1.0, 6.0, ((1, 8), (2, 16))),
        "material": with_ends(jax.random.randint(streams_of[2], (NX, NY, NZ), 0, NMAT), jax.random.fold_in(streams_of[2], 1), 0, NMAT - 1).astype(jnp.int32),
        "inv_eps": jnp.clip(jnp.exp(jax.random.uniform(streams_of[3], (NMAT,), jnp.float32, math.log(0.08), math.log(1.0))), 0.08, 1.0),
        "forward_design": centred(streams_of[4], (3, NX, NY, DZ), 1.0, 6.0, ((1, 8), (2, 16))),
        "cell_slot": draw_cell_slot(jax.random.fold_in(streams_of[8], 71), 0),
        "tile_pillars": draw_tile_pillars(jax.random.fold_in(streams_of[8], 71), 0),
        "pillar_rank": draw_pillar_rank(jax.random.fold_in(streams_of[8], 71), 0),
    }


courant = 0.5
grad_scale = 0.125


def next_cell(field, axis):
    rest = lax.slice_in_dim(field, 1, field.shape[axis], axis=axis)
    edge = jnp.zeros_like(lax.slice_in_dim(field, 0, 1, axis=axis))
    return jnp.concatenate([rest, edge], axis=axis)


def prior_cell(field, axis):
    rest = lax.slice_in_dim(field, 0, field.shape[axis] - 1, axis=axis)
    edge = jnp.zeros_like(lax.slice_in_dim(field, 0, 1, axis=axis))
    return jnp.concatenate([edge, rest], axis=axis)


def material_coefficient(material, inv_eps):
    coefficient = jnp.zeros(material.shape, jnp.float32)
    for which in range(inv_eps.shape[0]):
        coefficient = coefficient + jnp.where(material == which, inv_eps[which], jnp.zeros((), jnp.float32))
    return courant * coefficient


def reference(adjoint_e, adjoint_h, material, inv_eps, forward_design, cell_slot, tile_pillars, pillar_rank):
    efield_x = adjoint_e[0].astype(jnp.float32)
    efield_y = adjoint_e[1].astype(jnp.float32)
    efield_z = adjoint_e[2].astype(jnp.float32)
    hnew_x = adjoint_h[0].astype(jnp.float32) - courant * ((next_cell(efield_z, 1) - efield_z) - (next_cell(efield_y, 2) - efield_y))
    hnew_y = adjoint_h[1].astype(jnp.float32) - courant * ((next_cell(efield_x, 2) - efield_x) - (next_cell(efield_z, 0) - efield_z))
    hnew_z = adjoint_h[2].astype(jnp.float32) - courant * ((next_cell(efield_y, 0) - efield_y) - (next_cell(efield_x, 1) - efield_x))
    new_h = lax.optimization_barrier(jnp.stack([hnew_x, hnew_y, hnew_z]).astype(jnp.bfloat16))
    magnetic_x = new_h[0].astype(jnp.float32)
    magnetic_y = new_h[1].astype(jnp.float32)
    magnetic_z = new_h[2].astype(jnp.float32)
    coefficient = material_coefficient(material, inv_eps)
    enew_x = efield_x + coefficient * ((magnetic_z - prior_cell(magnetic_z, 1)) - (magnetic_y - prior_cell(magnetic_y, 2)))
    enew_y = efield_y + coefficient * ((magnetic_x - prior_cell(magnetic_x, 2)) - (magnetic_z - prior_cell(magnetic_z, 0)))
    enew_z = efield_z + coefficient * ((magnetic_y - prior_cell(magnetic_y, 0)) - (magnetic_x - prior_cell(magnetic_x, 1)))
    new_e = jnp.stack([enew_x, enew_y, enew_z]).astype(jnp.bfloat16)
    offset = (NZ - DZ) // 2
    slab = lax.slice_in_dim(adjoint_e, offset, offset + DZ, axis=3).astype(jnp.float32)
    intersection_density = jnp.sum(slab * forward_design.astype(jnp.float32), axis=0)
    layer_sums = intersection_density.reshape(NX, NY, DL, DZ // DL).sum(axis=3)
    tile_x = (jnp.arange(NX) // CX).astype(jnp.int32)
    tile_y = (jnp.arange(NY) // CY).astype(jnp.int32)
    pillar_of = tile_pillars[tile_x[:, None], tile_y[None, :], cell_slot]
    pillar_sums = jax.ops.segment_sum(layer_sums.reshape(NX * NY, DL), pillar_of.reshape(-1), num_segments=P_SIZE)
    gradient = jnp.zeros((DL, P_SIZE), jnp.float32).at[:, pillar_rank].set(grad_scale * pillar_sums.T)
    return new_e, new_h, gradient
```

```python
import jax
import jax.numpy as jnp
from jax import lax
from jax.experimental import pallas as pl
from jax.experimental.pallas import tpu as pltpu
from jax.sharding import PartitionSpec as P

F32, BF16, I32 = jnp.float32, jnp.bfloat16, jnp.int32
ANY = pl.BlockSpec(memory_space=pl.ANY)
VM = pl.BlockSpec(memory_space=pltpu.VMEM)
SM = pl.BlockSpec(memory_space=pltpu.SMEM)
DL = 32
CHUNKS = 8


def split(v):
    hi = v.astype(BF16)
    return hi, (v - hi.astype(F32)).astype(BF16)


def iota(shape, axis):
    return lax.broadcasted_iota(I32, shape, axis)


def dot(a, b):
    return jnp.dot(a, b, preferred_element_type=F32)


def pillar_kernel(
    e_hbm, h_hbm, f_hbm, slot_ref, tiles_hbm, rank_hbm,
    send_ref, xa_ref, xb_ref, ya_ref, yb_ref, c_ref, d_ref, y0_ref,
    e, f, hx, hy, tiles, rank, cells, acc, sem, fsem, msem,
):
    gx, gy = lax.axis_index("gx"), lax.axis_index("gy")
    _, nx, ny, nz = e.shape
    step = nx // CHUNKS
    copies = []
    for i in range(CHUNKS):
        part = pl.ds(i * step, step)
        copies.append((
            pltpu.make_async_copy(e_hbm.at[:, part], e.at[:, part], sem.at[i]),
            pltpu.make_async_copy(f_hbm.at[:, part], f.at[:, part], fsem.at[i]),
        ))
    extra = [
        pltpu.make_async_copy(tiles_hbm.at[gx, pl.ds(gy // 8 * 8, 8)], tiles, msem.at[0]),
        pltpu.make_async_copy(rank_hbm.at[pl.ds(gx * 64, 64)], rank, msem.at[1]),
        pltpu.make_async_copy(h_hbm.at[pl.ds(1, 2), nx - 1], hx, msem.at[2]),
        pltpu.make_async_copy(h_hbm.at[0, :, pl.ds(ny - 8, 8)], hy.at[0], msem.at[3]),
        pltpu.make_async_copy(h_hbm.at[2, :, pl.ds(ny - 8, 8)], hy.at[1], msem.at[4]),
    ]
    for one, two in copies[:1]:
        one.start()
        two.start()
    for one in extra:
        one.start()
    for one, two in copies[1:]:
        one.start()
        two.start()

    cells[:, :ny] = slot_ref[...]
    cells[:, ny:] = slot_ref[...]
    half = nx // 2
    lane = iota((half, 2 * ny), 1)
    pair = jnp.where(lane < ny, cells[pl.ds(0, half, stride=2), :], cells[pl.ds(1, half, stride=2), :])

    extra[0].wait()
    extra[1].wait()
    own = jnp.sum(jnp.where(iota(tiles.shape, 0) == gy % 8, tiles[...], 0), axis=0, keepdims=True)
    along_x = own // 512 - gx * 16
    along_y = own % 512 - gy * 32
    quarter = gy // 4
    ranks = jnp.zeros((16, 128), I32)
    for q in range(4):
        ranks = jnp.where(quarter == q, rank[pl.ds(q, 16, stride=4), :], ranks)
    turned = ranks
    for q in range(1, 4):
        turned = jnp.where(gy % 4 == q, pltpu.roll(ranks, 128 - 32 * q, 1), turned)
    square = jnp.concatenate([turned, jnp.zeros((112, 128), I32)], axis=0)
    columns = jnp.transpose(square)[:32]
    slots = own.shape[1]
    found = jnp.zeros((32, slots), I32)
    for q in range(16):
        found = jnp.where(along_x == q, columns[:, q : q + 1], found)
    my_rank = jnp.sum(jnp.where(iota((32, slots), 0) == along_y, found, 0), axis=0, keepdims=True)
    below = jnp.zeros((32, slots), I32)
    for q in range(16):
        below = below + jnp.where(columns[:, q : q + 1] < my_rank, 1, 0)
    order = jnp.sum(below, axis=0, keepdims=True)
    row = jnp.where(own >= 0, (order & 3) * 128 + (order >> 2), -1)
    place = (my_rank & 511).astype(F32)

    acc[...] = jnp.zeros(acc.shape, F32)
    for i, (one, two) in enumerate(copies):
        one.wait()
        two.wait()
        part = pl.ds(i * step, step)
        density = jnp.zeros((step * ny, nz), F32)
        for c in range(3):
            density = density + (
                e[c, part].astype(F32) * f[c, part].astype(F32)
            ).reshape(step * ny, nz)
        hi, lo = split(density)
        both = jnp.concatenate([hi, lo], axis=1)
        hot = jnp.concatenate(
            [
                jnp.where(iota((slots, 128), 0) == pair[p : p + 1], 1.0, 0.0).astype(BF16)
                for p in range(i * step // 2, (i + 1) * step // 2)
            ],
            axis=1,
        )
        acc[...] += dot(hot, both)

    sums = acc[:, :nz] + acc[:, nz:]
    hi, lo = split(sums)
    match = iota((slots, slots), 0) == row
    moved = dot(jnp.where(match, 1.0, 0.0).astype(BF16), jnp.concatenate([hi, lo], axis=1))
    moved = moved[:, :nz] + moved[:, nz:]
    spot = jnp.sum(jnp.where(match, place, 0.0), axis=1, keepdims=True)
    lanes = iota((128, 128), 1)
    values, spots = jnp.zeros((128, 128), F32), jnp.zeros((128, 128), F32)
    for k in range(4):
        hi, lo = split(moved[k * 128 : (k + 1) * 128])
        gather = jnp.where(lanes == 32 * k + iota((128, 128), 0) // 4, 0.125, 0.0).astype(BF16)
        values = values + dot(hi, gather) + dot(lo, gather)
        spots = jnp.where(lanes == k, spot[k * 128 : (k + 1) * 128], spots)
    send_ref[pl.ds(0, 128, stride=2), :] = values
    send_ref[pl.ds(1, 128, stride=2), :] = spots

    for one in extra[2:]:
        one.wait()

    def face(c, y):
        base = y // 8 * 8
        return e[c, :, pl.ds(base, 8), :].astype(F32)[:, y - base, :]

    y0x, y0z, y0y = face(0, 0), face(2, 0), None
    y0_ref[0] = y0x
    y0_ref[1] = y0z
    last = ny - 1
    up_y = [face(0, last), face(1, last), face(2, last)]
    up_y += [hy[0].astype(F32)[:, 7, :], hy[1].astype(F32)[:, 7, :]]

    def pack_x(up_ref, down_ref):
        for c in range(3):
            up_ref[c] = e[c, nx - 1]
        up_ref[3] = hx[0]
        up_ref[4] = hx[1]
        down_ref[0] = e[1, 0]
        down_ref[1] = e[2, 0]
        for c in range(2, 5):
            down_ref[c] = jnp.zeros((ny, nz), BF16)

    def pack_y(up_ref, down_ref):
        for c in range(5):
            up_ref[c] = up_y[c].astype(BF16)
        down_ref[0] = y0x.astype(BF16)
        down_ref[1] = y0z.astype(BF16)
        for c in range(2, 5):
            down_ref[c] = jnp.zeros((nx, nz), BF16)

    def pack_corner(up_ref, down_ref):
        up_ref[...] = jnp.broadcast_to(y0x[nx - 1 : nx], (8, nz))
        down_ref[...] = jnp.broadcast_to(up_y[1][0:1], (8, nz))

    @pl.when(gx % 2 == 0)
    def _():
        pack_x(xa_ref, xb_ref)
        pack_corner(c_ref, d_ref)

    @pl.when(gx % 2 == 1)
    def _():
        pack_x(xb_ref, xa_ref)
        pack_corner(d_ref, c_ref)

    @pl.when(gy % 2 == 0)
    def _():
        pack_y(ya_ref, yb_ref)

    @pl.when(gy % 2 == 1)
    def _():
        pack_y(yb_ref, ya_ref)


def field_kernel(
    e_hbm, h_hbm, m_hbm, eps_ref, xa_ref, xb_ref, ya_ref, yb_ref, c_ref, d_ref, y0_ref,
    ne_hbm, nh_hbm,
    e, h, m, ne, nh, yup, ylow, sem, hsem, msem, esem, osem,
):
    gx, gy = lax.axis_index("gx"), lax.axis_index("gy")
    _, nx, ny, nz = h.shape
    step = nx // CHUNKS
    loads = []
    for i in range(CHUNKS):
        part = pl.ds(i * step, step)
        loads.append((
            pltpu.make_async_copy(e_hbm.at[:, part], e.at[:, part], sem.at[i]),
            pltpu.make_async_copy(h_hbm.at[:, part], h.at[:, part], hsem.at[i]),
            pltpu.make_async_copy(m_hbm.at[part], m.at[part], msem.at[i]),
        ))
    for group in loads:
        for one in group:
            one.start()
    stores = []
    for i in range(CHUNKS):
        part = pl.ds(i * step, step)
        stores.append((
            pltpu.make_async_copy(nh.at[:, part], nh_hbm.at[:, part], osem.at[i]),
            pltpu.make_async_copy(ne.at[:, part], ne_hbm.at[:, part], esem.at[i]),
        ))

    even_x, even_y = gx % 2 == 0, gy % 2 == 0
    last_lane = iota((ny, nz), 1) == nz - 1
    first_lane = iota((ny, nz), 1) == 0
    last_row = iota((ny, nz), 0) == ny - 1
    first_row = iota((ny, nz), 0) == 0

    def up_z(v):
        return jnp.where(iota(v.shape, 1) == nz - 1, 0.0, pltpu.roll(v, nz - 1, 1))

    def low_z(v):
        return jnp.where(iota(v.shape, 1) == 0, 0.0, pltpu.roll(v, 1, 1))

    def up_y(v, edge):
        n = v.shape[0]
        return jnp.where(iota(v.shape, 0) == n - 1, edge, pltpu.roll(v, n - 1, 0))

    def low_y(v, edge):
        return jnp.where(iota(v.shape, 0) == 0, edge, pltpu.roll(v, 1, 0))

    def either(flag, a, b):
        return jnp.where(flag, a.astype(F32), b.astype(F32))

    for c in range(2):
        e[c + 1, nx] = either(even_x, xa_ref[c], xb_ref[c]).astype(BF16)
        yup[c] = either(even_y, ya_ref[c], yb_ref[c])
    ly = [either(even_y, yb_ref[c], ya_ref[c]) for c in range(5)]
    edge = jnp.where(even_x, c_ref[0:1], d_ref[0:1])
    inside = jnp.where(gy > 0, 1.0, 0.0)
    ex, ey, ez, hx, hz = ly
    ylow[0] = (inside * (hx - 0.5 * ((y0_ref[1] - ez) - (up_z(ey) - ey)))).astype(BF16).astype(F32)
    ylow[1] = (inside * (hz - 0.5 * ((up_y(ey, edge) - ey) - (y0_ref[0] - ex)))).astype(BF16).astype(F32)
    for one in loads[0]:
        one.wait()
    ex, ey, ez, hy, hz = [either(even_x, xb_ref[c], xa_ref[c]) for c in range(5)]
    edge = jnp.where(even_x, d_ref[0:1], c_ref[0:1])
    inside = jnp.where(gx > 0, 1.0, 0.0)
    e0y, e0z = e[1, 0].astype(F32), e[2, 0].astype(F32)
    hy_low = (inside * (hy - 0.5 * ((up_z(ex) - ex) - (e0z - ez)))).astype(BF16)
    hz_low = (inside * (hz - 0.5 * ((e0y - ey) - (up_y(ex, edge) - ex)))).astype(BF16)

    coefs = [0.5 * eps_ref[k] for k in range(4)]

    def plane(x, carry):
        hy_low, hz_low = carry
        ex, ey, ez = [e[c, x].astype(F32) for c in range(3)]
        eyn, ezn = e[1, x + 1].astype(F32), e[2, x + 1].astype(F32)
        upx, upz = yup[0, pl.ds(x, 1)], yup[1, pl.ds(x, 1)]
        bx = (h[0, x].astype(F32) - 0.5 * ((up_y(ez, upz) - ez) - (up_z(ey) - ey))).astype(BF16)
        by = (h[1, x].astype(F32) - 0.5 * ((up_z(ex) - ex) - (ezn - ez))).astype(BF16)
        bz = (h[2, x].astype(F32) - 0.5 * ((eyn - ey) - (up_y(ex, upx) - ex))).astype(BF16)
        nh[0, x] = bx
        nh[1, x] = by
        nh[2, x] = bz
        hx, hy, hz = bx.astype(F32), by.astype(F32), bz.astype(F32)
        mat = m[x]
        coef = jnp.where(mat == 0, coefs[0], jnp.where(mat == 1, coefs[1], jnp.where(mat == 2, coefs[2], coefs[3])))
        lowx, lowz = ylow[0, pl.ds(x, 1)], ylow[1, pl.ds(x, 1)]
        ne[0, x] = (ex + coef * ((hz - low_y(hz, lowz)) - (hy - low_z(hy)))).astype(BF16)
        ne[1, x] = (ey + coef * ((hx - low_z(hx)) - (hz - hz_low.astype(F32)))).astype(BF16)
        ne[2, x] = (ez + coef * ((hy - hy_low.astype(F32)) - (hx - low_y(hx, lowx)))).astype(BF16)
        return by, bz

    carry = (hy_low, hz_low)
    for i in range(CHUNKS):
        if i + 1 < CHUNKS:
            for one in loads[i + 1]:
                one.wait()
        carry = lax.fori_loop(i * step, (i + 1) * step, plane, carry)
        for one in stores[i]:
            one.start()
    for group in stores:
        for one in group:
            one.wait()


def place_kernel(got_ref, grad_ref):
    values = jnp.transpose(got_ref[pl.ds(0, 128, stride=2), :])
    spots = got_ref[pl.ds(1, 128, stride=2), :].astype(I32)
    ranks = grad_ref.shape[1]
    total = jnp.zeros((2 * DL, ranks), F32)
    for k in range(4):
        hot = jnp.where(iota((128, ranks), 1) == spots[:, k : k + 1], 1.0, 0.0).astype(BF16)
        hi, lo = split(values[k * DL : (k + 1) * DL])
        total = total + dot(jnp.concatenate([hi, lo], axis=0), hot)
    grad_ref[...] = total[:DL] + total[DL:]


def per_device(
    adjoint_e, adjoint_h, material, inv_eps, forward_design, cell_slot, tile_pillars, pillar_rank
):
    _, nx, ny, nz = adjoint_e.shape
    sx, sy = lax.axis_size("gx"), lax.axis_size("gy")
    both = ("gx", "gy")
    params = pltpu.CompilerParams(vmem_limit_bytes=40 * 1024 * 1024)
    shape = jax.ShapeDtypeStruct
    send, xa, xb, ya, yb, c, d, y0 = pl.pallas_call(
        pillar_kernel,
        out_shape=(
            shape((256, 128), F32),
            shape((5, ny, nz), BF16), shape((5, ny, nz), BF16),
            shape((5, nx, nz), BF16), shape((5, nx, nz), BF16),
            shape((8, nz), F32), shape((8, nz), F32),
            shape((2, nx, nz), F32),
        ),
        in_specs=[ANY, ANY, ANY, VM, ANY, ANY],
        out_specs=[VM] * 8,
        scratch_shapes=[
            pltpu.VMEM((3, nx, ny, nz), BF16), pltpu.VMEM((3, nx, ny, nz), BF16),
            pltpu.VMEM((2, ny, nz), BF16), pltpu.VMEM((2, nx, 8, nz), BF16),
            pltpu.VMEM((8, 512), I32), pltpu.VMEM((64, 128), I32),
            pltpu.VMEM((nx, 2 * ny), I32), pltpu.VMEM((512, 2 * nz), F32),
            pltpu.SemaphoreType.DMA((CHUNKS,)), pltpu.SemaphoreType.DMA((CHUNKS,)),
            pltpu.SemaphoreType.DMA((5,)),
        ],
        compiler_params=params,
        name="pillars",
    )(adjoint_e, adjoint_h, forward_design, cell_slot, tile_pillars, pillar_rank.reshape(512, 128))

    got = lax.all_to_all(send.reshape(128, 2, 128), both, 0, 0, tiled=True).reshape(256, 128)

    def swap(v, axis, size, low):
        pairs = []
        for i in range(low, size - 1, 2):
            pairs += [(i, i + 1), (i + 1, i)]
        return lax.ppermute(v, axis, pairs)

    def swap_corner(v, low):
        pairs = []
        for i in range(low, sx - 1, 2):
            for j in range(1, sy):
                one, two = i * sy + j, (i + 1) * sy + j - 1
                pairs += [(one, two), (two, one)]
        return lax.ppermute(v, both, pairs)

    xa, xb = swap(xa, "gx", sx, 0), swap(xb, "gx", sx, 1)
    ya, yb = swap(ya, "gy", sy, 0), swap(yb, "gy", sy, 1)
    c, d = swap_corner(c, 0), swap_corner(d, 1)

    new_e, new_h = pl.pallas_call(
        field_kernel,
        out_shape=(shape(adjoint_e.shape, BF16), shape(adjoint_e.shape, BF16)),
        in_specs=[ANY, ANY, ANY, SM] + [VM] * 7,
        out_specs=[ANY, ANY],
        scratch_shapes=[
            pltpu.VMEM((3, nx + 1, ny, nz), BF16), pltpu.VMEM((3, nx, ny, nz), BF16),
            pltpu.VMEM((nx, ny, nz), I32),
            pltpu.VMEM((3, nx, ny, nz), BF16), pltpu.VMEM((3, nx, ny, nz), BF16),
            pltpu.VMEM((2, nx, nz), F32), pltpu.VMEM((2, nx, nz), F32),
        ] + [pltpu.SemaphoreType.DMA((CHUNKS,))] * 5,
        compiler_params=params,
        name="fields",
    )(adjoint_e, adjoint_h, material, inv_eps, xa, xb, ya, yb, c, d, y0)

    gradient = pl.pallas_call(
        place_kernel,
        out_shape=shape((DL, 512), F32),
        in_specs=[VM],
        out_specs=VM,
        compiler_params=params,
        name="place",
    )(got)
    return new_e, new_h, gradient


def solution(mesh):
    return jax.shard_map(
        per_device,
        mesh=mesh,
        in_specs=(
            P(None, "gx", "gy", None),
            P(None, "gx", "gy", None),
            P("gx", "gy", None),
            P(),
            P(None, "gx", "gy", None),
            P("gx", "gy"),
            P(),
            P(),
        ),
        out_specs=(P(None, "gx", "gy", None), P(None, "gx", "gy", None), P(None, ("gx", "gy"))),
        check_vma=False,
    )
```

```python
import jax
import jax.numpy as jnp
from jax import lax
from jax.experimental import pallas as pl
from jax.experimental.pallas import tpu as pltpu
from jax.sharding import PartitionSpec as P

F32, BF16, I32 = jnp.float32, jnp.bfloat16, jnp.int32
HBM = pl.BlockSpec(memory_space=pltpu.HBM)
VM = pl.BlockSpec(memory_space=pltpu.VMEM)
SM = pl.BlockSpec(memory_space=pltpu.SMEM)
DL = 32
CHUNKS = 8


def split(v):
    hi = v.astype(BF16)
    return hi, (v - hi.astype(F32)).astype(BF16)


def iota(shape, axis):
    return lax.broadcasted_iota(I32, shape, axis)


def dot(a, b):
    return jnp.dot(a, b, preferred_element_type=F32)


def face_kernel(e_hbm, h_hbm, a_ref, b_ref, sem):
    gx = lax.axis_index("gx")
    last = e_hbm.shape[1] - 1

    def fill(up_ref, down_ref):
        copies = [
            pltpu.make_async_copy(e_hbm.at[:, last], up_ref.at[pl.ds(0, 3)], sem.at[0]),
            pltpu.make_async_copy(h_hbm.at[pl.ds(1, 2), last], up_ref.at[pl.ds(3, 2)], sem.at[1]),
            pltpu.make_async_copy(e_hbm.at[pl.ds(1, 2), 0], down_ref.at[pl.ds(0, 2)], sem.at[2]),
        ]
        for one in copies:
            one.start()
        down_ref[pl.ds(2, 3)] = jnp.zeros((3,) + down_ref.shape[1:], BF16)
        for one in copies:
            one.wait()

    @pl.when(gx % 2 == 0)
    def _():
        fill(a_ref, b_ref)

    @pl.when(gx % 2 == 1)
    def _():
        fill(b_ref, a_ref)


def pillar_kernel(
    e_hbm, h_hbm, f_hbm, slot_hbm, tiles_hbm, rank_hbm,
    send_ref, ya_ref, yb_ref, y0_ref,
    e, f, hy, tiles, rank, slot, cells, acc, sem, fsem, msem,
):
    gx, gy = lax.axis_index("gx"), lax.axis_index("gy")
    _, nx, ny, nz = e.shape
    step = nx // CHUNKS
    copies = []
    for i in range(CHUNKS):
        part = pl.ds(i * step, step)
        copies.append((
            pltpu.make_async_copy(e_hbm.at[:, part], e.at[:, part], sem.at[i]),
            pltpu.make_async_copy(f_hbm.at[:, part], f.at[:, part], fsem.at[i]),
        ))
    extra = [
        pltpu.make_async_copy(tiles_hbm.at[gx, pl.ds(gy // 8 * 8, 8)], tiles, msem.at[0]),
        pltpu.make_async_copy(rank_hbm.at[pl.ds(gx * 64, 64)], rank, msem.at[1]),
        pltpu.make_async_copy(slot_hbm, slot, msem.at[2]),
        pltpu.make_async_copy(h_hbm.at[0, :, pl.ds(ny - 8, 8)], hy.at[0], msem.at[3]),
        pltpu.make_async_copy(h_hbm.at[2, :, pl.ds(ny - 8, 8)], hy.at[1], msem.at[4]),
    ]
    for one in extra[:3]:
        one.start()
    for one, two in copies[:1]:
        one.start()
        two.start()
    for one in extra[3:]:
        one.start()
    for one, two in copies[1:]:
        one.start()
        two.start()

    extra[2].wait()
    cells[:, :ny] = slot[...]
    cells[:, ny:] = slot[...]
    half = nx // 2
    lane = iota((half, 2 * ny), 1)
    pair = jnp.where(lane < ny, cells[pl.ds(0, half, stride=2), :], cells[pl.ds(1, half, stride=2), :])

    extra[0].wait()
    extra[1].wait()
    own = jnp.sum(jnp.where(iota(tiles.shape, 0) == gy % 8, tiles[...], 0), axis=0, keepdims=True)
    along_x = own // 512 - gx * 16
    along_y = own % 512 - gy * 32
    quarter = gy // 4
    ranks = jnp.zeros((16, 128), I32)
    for q in range(4):
        ranks = jnp.where(quarter == q, rank[pl.ds(q, 16, stride=4), :], ranks)
    turned = ranks
    for q in range(1, 4):
        turned = jnp.where(gy % 4 == q, pltpu.roll(ranks, 128 - 32 * q, 1), turned)
    square = jnp.concatenate([turned, jnp.zeros((112, 128), I32)], axis=0)
    columns = jnp.transpose(square)[:32]
    slots = own.shape[1]
    found = jnp.zeros((32, slots), I32)
    for q in range(16):
        found = jnp.where(along_x == q, columns[:, q : q + 1], found)
    my_rank = jnp.sum(jnp.where(iota((32, slots), 0) == along_y, found, 0), axis=0, keepdims=True)
    below = jnp.zeros((32, slots), I32)
    for q in range(16):
        below = below + jnp.where(columns[:, q : q + 1] < my_rank, 1, 0)
    order = jnp.sum(below, axis=0, keepdims=True)
    row = jnp.where(own >= 0, (order & 3) * 128 + (order >> 2), -1)
    place = (my_rank & 511).astype(F32)

    acc[...] = jnp.zeros(acc.shape, F32)
    for i, (one, two) in enumerate(copies):
        one.wait()
        two.wait()
        part = pl.ds(i * step, step)
        density = jnp.zeros((step * ny, nz), F32)
        for c in range(3):
            density = density + (
                e[c, part].astype(F32) * f[c, part].astype(F32)
            ).reshape(step * ny, nz)
        hi, lo = split(density)
        both = jnp.concatenate([hi, lo], axis=1)
        hot = jnp.concatenate(
            [
                jnp.where(iota((slots, 128), 0) == pair[p : p + 1], 1.0, 0.0).astype(BF16)
                for p in range(i * step // 2, (i + 1) * step // 2)
            ],
            axis=1,
        )
        acc[...] += dot(hot, both)

    sums = acc[:, :nz] + acc[:, nz:]
    hi, lo = split(sums)
    match = iota((slots, slots), 0) == row
    moved = dot(jnp.where(match, 1.0, 0.0).astype(BF16), jnp.concatenate([hi, lo], axis=1))
    moved = moved[:, :nz] + moved[:, nz:]
    spot = jnp.sum(jnp.where(match, place, 0.0), axis=1, keepdims=True)
    lanes = iota((128, 128), 1)
    values, spots = jnp.zeros((128, 128), F32), jnp.zeros((128, 128), F32)
    for k in range(4):
        hi, lo = split(moved[k * 128 : (k + 1) * 128])
        gather = jnp.where(lanes == 32 * k + iota((128, 128), 0) // 4, 0.125, 0.0).astype(BF16)
        values = values + dot(hi, gather) + dot(lo, gather)
        spots = jnp.where(lanes == k, spot[k * 128 : (k + 1) * 128], spots)
    send_ref[pl.ds(0, 128, stride=2), :] = values
    send_ref[pl.ds(1, 128, stride=2), :] = spots

    for one in extra[3:]:
        one.wait()

    def face(c, y):
        base = y // 8 * 8
        return e[c, :, pl.ds(base, 8), :].astype(F32)[:, y - base, :]

    y0x, y0z = face(0, 0), face(2, 0)
    y0_ref[0] = y0x
    y0_ref[1] = y0z
    last = ny - 1
    up_y = [face(0, last), face(1, last), face(2, last)]
    up_y += [hy[0].astype(F32)[:, 7, :], hy[1].astype(F32)[:, 7, :]]

    def pack(up_ref, down_ref):
        for c in range(5):
            up_ref[pl.ds(c * nx, nx)] = up_y[c].astype(BF16)
        down_ref[pl.ds(0, nx)] = y0x.astype(BF16)
        down_ref[pl.ds(nx, nx)] = y0z.astype(BF16)
        down_ref[pl.ds(2 * nx, 3 * nx)] = jnp.zeros((3 * nx, nz), BF16)
        up_ref[pl.ds(5 * nx, 16)] = jnp.zeros((16, nz), BF16)
        down_ref[pl.ds(5 * nx, 16)] = jnp.zeros((16, nz), BF16)

    @pl.when(gy % 2 == 0)
    def _():
        pack(ya_ref, yb_ref)

    @pl.when(gy % 2 == 1)
    def _():
        pack(yb_ref, ya_ref)


def field_kernel(
    e_hbm, h_hbm, m_hbm, eps_ref, xa_ref, xb_ref, ya_ref, yb_ref, y0_ref,
    ne_hbm, nh_hbm,
    e, h, m, ne, nh, ef, gf, sem, hsem, msem, esem, osem,
):
    gx, gy = lax.axis_index("gx"), lax.axis_index("gy")
    _, nx, ny, nz = h.shape
    step = nx // CHUNKS
    loads, stores = [], []
    for i in range(CHUNKS):
        part = pl.ds(i * step, step)
        loads.append((
            pltpu.make_async_copy(e_hbm.at[:, part], e.at[:, part], sem.at[i]),
            pltpu.make_async_copy(h_hbm.at[:, part], h.at[:, part], hsem.at[i]),
            pltpu.make_async_copy(m_hbm.at[part], m.at[part], msem.at[i]),
        ))
        stores.append((
            pltpu.make_async_copy(nh.at[:, part], nh_hbm.at[:, part], osem.at[i]),
            pltpu.make_async_copy(ne.at[:, part], ne_hbm.at[:, part], esem.at[i]),
        ))
    for group in loads:
        for one in group:
            one.start()

    even_x, even_y = gx % 2 == 0, gy % 2 == 0

    def up_z(v):
        return jnp.where(iota(v.shape, 1) == nz - 1, 0.0, pltpu.roll(v, nz - 1, 1))

    def up_row(v, edge):
        n = v.shape[0]
        return jnp.where(iota(v.shape, 0) == n - 1, edge, pltpu.roll(v, n - 1, 0))

    def either(flag, a, b):
        return jnp.where(flag, a.astype(F32), b.astype(F32))

    def rounded(v):
        return v.astype(BF16).astype(F32)

    ex, ey, ez, hx, hz = [
        either(even_y, yb_ref[pl.ds(c * nx, nx)], ya_ref[pl.ds(c * nx, nx)]) for c in range(5)
    ]
    corner = pl.ds(5 * nx, 16)
    below, above = either(even_y, yb_ref[corner], ya_ref[corner]), either(even_y, ya_ref[corner], yb_ref[corner])
    inside = jnp.where(gy > 0, 1.0, 0.0)
    low_x = rounded(inside * (2.0 * hx - ((y0_ref[1] - ez) - (up_z(ey) - ey))))
    low_z = rounded(inside * (2.0 * hz - ((up_row(ey, below[0:1]) - ey) - (y0_ref[0] - ex))))
    high_x = either(even_y, ya_ref[pl.ds(0, nx)], yb_ref[pl.ds(0, nx)])
    high_z = either(even_y, ya_ref[pl.ds(nx, nx)], yb_ref[pl.ds(nx, nx)])
    for x in range(nx):
        ef[0, x, pl.ds(ny, 1)] = high_x[x : x + 1]
        ef[2, x, pl.ds(ny, 1)] = high_z[x : x + 1]
        gf[0, x + 1, pl.ds(7, 1)] = low_x[x : x + 1]
        gf[2, x + 1, pl.ds(7, 1)] = low_z[x : x + 1]
    rows, kept = pl.ds(0, ny), pl.ds(8, ny)
    for c in range(2):
        ef[c + 1, nx, rows] = either(even_x, xa_ref[c], xb_ref[c])
    ex, ey, ez, hy, hz = [either(even_x, xb_ref[c], xa_ref[c]) for c in range(5)]
    inside = jnp.where(gx > 0, 1.0, 0.0)
    for one in loads[0]:
        one.wait()
    for c in range(3):
        ef[c, 0, rows] = e[c, 0].astype(F32)
    gf[1, 0, kept] = rounded(inside * (2.0 * hy - ((up_z(ex) - ex) - (ef[2, 0, rows] - ez))))
    gf[2, 0, kept] = rounded(inside * (2.0 * hz - ((ef[1, 0, rows] - ey) - (up_row(ex, above[0:1]) - ex))))

    row, col = iota((nz, nz), 0), iota((nz, nz), 1)
    eye = jnp.where(row == col, 1.0, 0.0)
    ahead = jnp.where(row == col + 1, 1.0, 0.0) - eye
    back = eye - jnp.where(row == col - 1, 1.0, 0.0)
    none = jnp.zeros((nz, nz), F32)
    wx = jnp.concatenate([2.0 * eye, ahead], axis=0).astype(BF16)
    wy = jnp.concatenate([2.0 * eye, -ahead], axis=0).astype(BF16)
    wz = jnp.concatenate([2.0 * eye, -eye], axis=0).astype(BF16)
    wb = jnp.concatenate(
        [jnp.concatenate([back, none], axis=1), jnp.concatenate([none, back], axis=1)], axis=0
    ).astype(BF16)
    lane = iota((ny, nz), 1)
    table = jnp.zeros((ny, nz), F32)
    for k in range(4):
        table = jnp.where(lane == k, 0.25 * eps_ref[k], table)

    def first(x):
        if x + 1 < nx:
            for c in range(3):
                ef[c, x + 1, rows] = e[c, x + 1].astype(F32)
        shifted = pl.ds(1, ny)
        fx = dot(jnp.concatenate([h[0, x], e[1, x]], axis=1), wx)
        fy = dot(jnp.concatenate([h[1, x], e[0, x]], axis=1), wy)
        fz = dot(jnp.concatenate([h[2, x], e[0, x]], axis=1), wz)
        ez = ef[2, x, rows]
        fx = fx - (ef[2, x, shifted] - ez)
        fy = fy + (ef[2, x + 1, rows] - ez)
        fz = fz + ef[0, x, shifted] - (ef[1, x + 1, rows] - ef[1, x, rows])
        for c, v in enumerate((fx, fy, fz)):
            g = v.astype(BF16)
            nh[c, x] = g * BF16(0.5)
            gf[c, x + 1, kept] = g.astype(F32)

    def second(x):
        shifted = pl.ds(7, ny)
        pair = jnp.concatenate([nh[0, x], nh[1, x]], axis=1)
        along = dot(pair, wb)
        gx_, gy_, gz_ = [gf[c, x + 1, kept] for c in range(3)]
        coef = jnp.take_along_axis(table, m[x], axis=1)
        tx = (gz_ - gf[2, x + 1, shifted]) - along[:, nz:]
        ty = along[:, :nz] - (gz_ - gf[2, x, kept])
        tz = (gy_ - gf[1, x, kept]) - (gx_ - gf[0, x + 1, shifted])
        for c, t in enumerate((tx, ty, tz)):
            ne[c, x] = (ef[c, x, rows] + coef * t).astype(BF16)

    wb = wb * BF16(2.0)
    for i in range(CHUNKS + 1):
        if i + 1 < CHUNKS:
            for one in loads[i + 1]:
                one.wait()
        for x in range(step):
            if i < CHUNKS:
                first(i * step + x)
            if i > 0:
                second((i - 1) * step + x)
        if i < CHUNKS:
            stores[i][0].start()
        if i > 0:
            stores[i - 1][1].start()
    for group in stores:
        for one in group:
            one.wait()


def place_kernel(got_ref, grad_ref):
    values = jnp.transpose(got_ref[pl.ds(0, 128, stride=2), :])
    spots = got_ref[pl.ds(1, 128, stride=2), :].astype(I32)
    ranks = grad_ref.shape[1]
    total = jnp.zeros((2 * DL, ranks), F32)
    for k in range(4):
        hot = jnp.where(iota((128, ranks), 1) == spots[:, k : k + 1], 1.0, 0.0).astype(BF16)
        hi, lo = split(values[k * DL : (k + 1) * DL])
        total = total + dot(jnp.concatenate([hi, lo], axis=0), hot)
    grad_ref[...] = total[:DL] + total[DL:]


def per_device(
    adjoint_e, adjoint_h, material, inv_eps, forward_design, cell_slot, tile_pillars, pillar_rank
):
    _, nx, ny, nz = adjoint_e.shape
    sx, sy = lax.axis_size("gx"), lax.axis_size("gy")
    both = ("gx", "gy")
    shape = jax.ShapeDtypeStruct

    def stay(v):
        return pltpu.with_memory_space_constraint(v, pltpu.HBM)

    ranks = pillar_rank.reshape(512, 128)
    adjoint_e, adjoint_h, material, forward_design, cell_slot, tile_pillars, ranks = map(
        stay, (adjoint_e, adjoint_h, material, forward_design, cell_slot, tile_pillars, ranks)
    )

    def params(mib):
        return pltpu.CompilerParams(vmem_limit_bytes=mib * 1024 * 1024)

    def swap(v, axis, size, low):
        pairs = []
        for i in range(low, size - 1, 2):
            pairs += [(i, i + 1), (i + 1, i)]
        return lax.ppermute(v, axis, pairs)

    xa, xb = pl.pallas_call(
        face_kernel,
        out_shape=(shape((5, ny, nz), BF16), shape((5, ny, nz), BF16)),
        in_specs=[HBM, HBM],
        out_specs=[VM, VM],
        scratch_shapes=[pltpu.SemaphoreType.DMA((3,))],
        compiler_params=params(4),
        name="faces",
    )(adjoint_e, adjoint_h)
    xa, xb = swap(xa, "gx", sx, 0), swap(xb, "gx", sx, 1)

    send, ya, yb, y0 = pl.pallas_call(
        pillar_kernel,
        out_shape=(
            shape((256, 128), F32),
            shape((5 * nx + 16, nz), BF16), shape((5 * nx + 16, nz), BF16),
            shape((2, nx, nz), F32),
        ),
        in_specs=[HBM] * 6,
        out_specs=[VM] * 4,
        scratch_shapes=[
            pltpu.VMEM((3, nx, ny, nz), BF16), pltpu.VMEM((3, nx, ny, nz), BF16),
            pltpu.VMEM((2, nx, 8, nz), BF16),
            pltpu.VMEM((8, 512), I32), pltpu.VMEM((64, 128), I32), pltpu.VMEM((nx, ny), I32),
            pltpu.VMEM((nx, 2 * ny), I32), pltpu.VMEM((512, 2 * nz), F32),
            pltpu.SemaphoreType.DMA((CHUNKS,)), pltpu.SemaphoreType.DMA((CHUNKS,)),
            pltpu.SemaphoreType.DMA((5,)),
        ],
        compiler_params=params(12),
        name="pillars",
    )(adjoint_e, adjoint_h, forward_design, cell_slot, tile_pillars, ranks)

    got = lax.all_to_all(send.reshape(128, 2, 128), both, 0, 0, tiled=True).reshape(256, 128)

    even_x, even_y = lax.axis_index("gx") % 2 == 0, lax.axis_index("gy") % 2 == 0
    up = jnp.where(even_x, xa[0, ny - 1 :], xb[0, ny - 1 :])
    down = jnp.where(even_x, xb[0, :1], xa[0, :1])
    ya = lax.dynamic_update_slice(ya, jnp.where(even_y, up, down), (5 * nx, 0))
    yb = lax.dynamic_update_slice(yb, jnp.where(even_y, down, up), (5 * nx, 0))
    ya, yb = swap(ya, "gy", sy, 0), swap(yb, "gy", sy, 1)

    new_e, new_h = pl.pallas_call(
        field_kernel,
        out_shape=(shape(adjoint_e.shape, BF16), shape(adjoint_e.shape, BF16)),
        in_specs=[HBM, HBM, HBM, SM] + [VM] * 5,
        out_specs=[HBM, HBM],
        scratch_shapes=[
            pltpu.VMEM((3, nx, ny, nz), BF16), pltpu.VMEM((3, nx, ny, nz), BF16),
            pltpu.VMEM((nx, ny, nz), I32),
            pltpu.VMEM((3, nx, ny, nz), BF16), pltpu.VMEM((3, nx, ny, nz), BF16),
            pltpu.VMEM((3, nx + 1, ny + 8, nz), F32), pltpu.VMEM((3, nx + 1, ny + 8, nz), F32),
        ] + [pltpu.SemaphoreType.DMA((CHUNKS,))] * 5,
        compiler_params=params(20),
        name="fields",
    )(adjoint_e, adjoint_h, material, inv_eps, xa, xb, ya, yb, y0)

    gradient = pl.pallas_call(
        place_kernel,
        out_shape=shape((DL, 512), F32),
        in_specs=[VM],
        out_specs=VM,
        compiler_params=params(4),
        name="place",
    )(got)
    return new_e, new_h, gradient


def solution(mesh):
    return jax.shard_map(
        per_device,
        mesh=mesh,
        in_specs=(
            P(None, "gx", "gy", None),
            P(None, "gx", "gy", None),
            P("gx", "gy", None),
            P(),
            P(None, "gx", "gy", None),
            P("gx", "gy"),
            P(),
            P(),
        ),
        out_specs=(P(None, "gx", "gy", None), P(None, "gx", "gy", None), P(None, ("gx", "gy"))),
        check_vma=False,
    )
```

```python
import jax
import jax.numpy as jnp
from jax import lax
from jax.experimental import pallas as pl
from jax.experimental.pallas import tpu as pltpu
from jax.sharding import PartitionSpec as P

F32, BF16, I32 = jnp.float32, jnp.bfloat16, jnp.int32
HBM = pl.BlockSpec(memory_space=pltpu.HBM)
VM = pl.BlockSpec(memory_space=pltpu.VMEM)
SM = pl.BlockSpec(memory_space=pltpu.SMEM)
DL = 32
CHUNKS = 8
PARTS = 4


def split(v):
    hi = v.astype(BF16)
    return hi, (v - hi.astype(F32)).astype(BF16)


def iota(shape, axis):
    return lax.broadcasted_iota(I32, shape, axis)


def dot(a, b):
    return jnp.dot(a, b, preferred_element_type=F32)


def face_kernel(e_hbm, h_hbm, a_ref, b_ref, sem):
    gx = lax.axis_index("gx")
    last = e_hbm.shape[1] - 1

    def fill(up_ref, down_ref):
        copies = [
            pltpu.make_async_copy(e_hbm.at[:, last], up_ref.at[pl.ds(0, 3)], sem.at[0]),
            pltpu.make_async_copy(h_hbm.at[pl.ds(1, 2), last], up_ref.at[pl.ds(3, 2)], sem.at[1]),
            pltpu.make_async_copy(e_hbm.at[pl.ds(1, 2), 0], down_ref.at[pl.ds(0, 2)], sem.at[2]),
        ]
        for one in copies:
            one.start()
        down_ref[pl.ds(2, 3)] = jnp.zeros((3,) + down_ref.shape[1:], BF16)
        for one in copies:
            one.wait()

    @pl.when(gx % 2 == 0)
    def _():
        fill(a_ref, b_ref)

    @pl.when(gx % 2 == 1)
    def _():
        fill(b_ref, a_ref)


def lookup(table, index):
    rows = index.shape[0]
    result = jnp.zeros(index.shape, table.dtype)
    for q in range(4):
        part = jnp.broadcast_to(table[q : q + 1], (rows, 128))
        taken = jnp.take_along_axis(part, index & 127, axis=1, mode="promise_in_bounds")
        result = jnp.where(index >> 7 == q, taken, result)
    return result


def pillar_kernel(
    e_hbm, h_hbm, f_hbm, slot_hbm, tiles_hbm, rank_hbm,
    send_ref, ya_ref, yb_ref, y0_ref,
    e, f, y_first, y_last, y_h, tiles, rank, slot, cells, ids, acc, sem, fsem, msem,
):
    gx, gy = lax.axis_index("gx"), lax.axis_index("gy")
    _, nx, ny, nz = e.shape
    parts = sem.shape[0]
    step = nx // parts
    copies = []
    for i in range(parts):
        part = pl.ds(i * step, step)
        copies.append((
            pltpu.make_async_copy(e_hbm.at[:, part], e.at[:, part], sem.at[i]),
            pltpu.make_async_copy(f_hbm.at[:, part], f.at[:, part], fsem.at[i]),
        ))
    extra = [
        pltpu.make_async_copy(tiles_hbm.at[gx, pl.ds(gy // 8 * 8, 8)], tiles, msem.at[0]),
        pltpu.make_async_copy(rank_hbm.at[pl.ds(gx * 64, 64)], rank, msem.at[1]),
        pltpu.make_async_copy(slot_hbm, slot, msem.at[2]),
        pltpu.make_async_copy(e_hbm.at[:, :, pl.ds(0, 8)], y_first, msem.at[3]),
        pltpu.make_async_copy(e_hbm.at[:, :, pl.ds(ny - 8, 8)], y_last, msem.at[4]),
        pltpu.make_async_copy(h_hbm.at[0, :, pl.ds(ny - 8, 8)], y_h.at[0], msem.at[5]),
        pltpu.make_async_copy(h_hbm.at[2, :, pl.ds(ny - 8, 8)], y_h.at[1], msem.at[6]),
    ]
    for one in extra[:3]:
        one.start()
    for one, two in copies[:1]:
        one.start()
        two.start()
    for one in extra[3:]:
        one.start()
    for one, two in copies[1:]:
        one.start()
        two.start()
    ids[...] = iota(ids.shape, 0)
    lanes, rows = iota((128, 128), 1), iota((128, 128), 0)

    for one in extra[:3]:
        one.wait()
    quarter = gy // 4
    ranks = rank[pl.ds(0, 16, stride=4), :]
    for q in range(1, 4):
        ranks = jnp.where(quarter == q, rank[pl.ds(q, 16, stride=4), :], ranks)
    turned = ranks
    for q in range(1, 4):
        turned = jnp.where(gy % 4 == q, pltpu.roll(ranks, 128 - 32 * q, 1), turned)
    moved = [turned] + [pltpu.roll(turned, 32 * q, 1) for q in range(1, 4)]
    lane = iota((1, 128), 1)
    own_rank = []
    for q in range(4):
        line = moved[0][4 * q : 4 * q + 1]
        for k in range(1, 4):
            line = jnp.where(lane >> 5 == k, moved[k][4 * q + k : 4 * q + k + 1], line)
        own_rank.append(line)
    owner = [line >> 9 for line in own_rank]
    hits = [rows == line for line in owner]
    ones = [jnp.where(hit, 1.0, 0.0).astype(BF16) for hit in hits]
    counter = jnp.concatenate(
        [jnp.where(rows < lanes, 1.0, 0.0), jnp.ones((128, 128), F32)], axis=1
    ).astype(BF16)
    before = jnp.zeros((128, 128), F32)
    turn = []
    for q in range(4):
        both = dot(ones[q], counter)
        count = both[:, :128] + before
        turn.append(jnp.sum(jnp.where(hits[q], count, 0.0), axis=0, keepdims=True).astype(I32))
        before = before + both[:, 128:]
    spots = []
    for q in range(4):
        place = own_rank[q] & 511
        eight = jnp.where(iota((16, 128), 0) < 4, place & 255, place & 256)
        mine = (iota((16, 128), 0) & 3 == turn[q]) & (iota((16, 128), 0) < 8)
        spots.append(jnp.where(mine, eight, 0).astype(F32).astype(BF16))
    spots = lax.dot_general(
        jnp.concatenate(ones, axis=1), jnp.concatenate(spots, axis=1),
        (((1,), (1,)), ((), ())), preferred_element_type=F32,
    )
    send_ref[pl.ds(1, 128, stride=2), :] = jnp.concatenate([spots, jnp.zeros((128, 112), F32)], axis=1)
    target = jnp.concatenate([turn[q] * 128 + owner[q] for q in range(4)], axis=0)
    own = jnp.sum(jnp.where(iota(tiles.shape, 0) == gy % 8, tiles[...], 0), axis=0, keepdims=True)
    own = jnp.concatenate([own[:, 128 * q : 128 * (q + 1)] for q in range(4)], axis=0)
    canon = ((own >> 9) & 15) * 32 + (own & 31)
    target = lookup(target, canon)
    cells[:, :ny] = slot[...]
    cells[:, ny:] = slot[...]
    half = nx // 2
    pair = jnp.where(
        iota((half, 2 * ny), 1) < ny,
        cells[pl.ds(0, half, stride=2), :], cells[pl.ds(1, half, stride=2), :],
    )
    pair = lookup(target, pair)

    for i, (one, two) in enumerate(copies):
        one.wait()
        two.wait()
        part = pl.ds(i * step, step)
        density = e[0, part].astype(F32) * f[0, part].astype(F32)
        for c in range(1, 3):
            density = density + e[c, part].astype(F32) * f[c, part].astype(F32)
        both = jnp.concatenate(split(density.reshape(step * ny, nz)), axis=1)
        hot = jnp.concatenate(
            [
                jnp.where(ids[...] == pair[p : p + 1], 1.0, 0.0).astype(BF16)
                for p in range(i * step // 2, (i + 1) * step // 2)
            ],
            axis=1,
        )
        total = dot(hot, both)
        if i == 0:
            acc[...] = total
        elif i + 1 < parts:
            acc[...] += total
    total = acc[...] + total
    values = jnp.zeros((128, 128), F32)
    for k in range(4):
        part = total[k * 128 : (k + 1) * 128]
        hi, lo = split(part[:, :nz] + part[:, nz:])
        gather = jnp.where(lanes == 32 * k + (rows >> 2), 0.125, 0.0).astype(BF16)
        values = values + dot(hi, gather) + dot(lo, gather)
    send_ref[pl.ds(0, 128, stride=2), :] = values

    for one in extra[3:]:
        one.wait()
    at = iota((nx, 8 * nx), 1) - 8 * iota((nx, 8 * nx), 0)
    low = jnp.where(at == 0, 1.0, 0.0).astype(BF16)
    high = jnp.where(at == 7, 1.0, 0.0).astype(BF16)

    def face(which, one, two):
        both = jnp.concatenate([one.reshape(8 * nx, nz), two.reshape(8 * nx, nz)], axis=1)
        both = dot(which, both)
        return both[:, :nz], both[:, nz:]

    y0x, y0z = face(low, y_first[0], y_first[2])
    up_y = face(high, y_last[0], y_last[1]) + face(high, y_last[2], y_h[0]) + face(high, y_h[1], y_h[1])[:1]
    y0_ref[0] = y0x
    y0_ref[1] = y0z

    def pack(up_ref, down_ref):
        for c in range(5):
            up_ref[pl.ds(c * nx, nx)] = up_y[c].astype(BF16)
        down_ref[pl.ds(0, nx)] = y0x.astype(BF16)
        down_ref[pl.ds(nx, nx)] = y0z.astype(BF16)
        down_ref[pl.ds(2 * nx, 3 * nx)] = jnp.zeros((3 * nx, nz), BF16)
        up_ref[pl.ds(5 * nx, 16)] = jnp.zeros((16, nz), BF16)
        down_ref[pl.ds(5 * nx, 16)] = jnp.zeros((16, nz), BF16)

    @pl.when(gy % 2 == 0)
    def _():
        pack(ya_ref, yb_ref)

    @pl.when(gy % 2 == 1)
    def _():
        pack(yb_ref, ya_ref)


def eye_like(distance, n):
    return jnp.where(iota((n, n), 0) == iota((n, n), 1) + distance, 1.0, 0.0)


def square(a, b, c, d):
    top, bottom = jnp.concatenate([a, b], axis=1), jnp.concatenate([c, d], axis=1)
    return jnp.concatenate([top, bottom], axis=0).astype(BF16)


def side(one, two):
    shape = (one.shape[0] * one.shape[1], one.shape[2])
    return jnp.concatenate([one.reshape(shape), two.reshape(shape)], axis=1)


def spread_kernel(e_hbm, h_hbm, ef_ref, hf_ref, e, h, sem, hsem):
    _, nx, ny, nz = h.shape
    parts = sem.shape[0]
    step = nx // parts
    loads = []
    for i in range(parts):
        part = pl.ds(i * step, step)
        loads.append((
            pltpu.make_async_copy(e_hbm.at[:, part], e.at[:, part], sem.at[i]),
            pltpu.make_async_copy(h_hbm.at[:, part], h.at[:, part], hsem.at[i]),
        ))
    for group in loads:
        for one in group:
            one.start()
    eye = eye_like(0, nz)
    ahead = eye_like(1, nz) - eye
    none = jnp.zeros((nz, nz), F32)
    wx = square(2.0 * eye, none, ahead, eye)
    wy = square(2.0 * eye, none, -ahead, eye)
    for i in range(parts):
        for one in loads[i]:
            one.wait()
        part = pl.ds(i * step, step)
        for c, other, w in ((0, 1, wx), (1, 0, wy)):
            both = dot(side(h[c, part], e[other, part]), w)
            for k in range(step):
                x = i * step + k
                line = both[k * ny : (k + 1) * ny]
                hf_ref[c, x] = line[:, :nz]
                ef_ref[other, x, pl.ds(0, ny)] = line[:, nz:]
        for k in range(step):
            x = i * step + k
            hz = h[2, x].astype(F32)
            hf_ref[2, x] = hz + hz
            ef_ref[2, x, pl.ds(0, ny)] = e[2, x].astype(F32)


def field_kernel(
    ef, hf, m_hbm, eps_ref, xa_ref, xb_ref, ya_ref, yb_ref, y0_ref,
    ne_hbm, nh_hbm,
    m, ne, nh, gf, high, beyond, msem, esem, osem,
):
    gx, gy = lax.axis_index("gx"), lax.axis_index("gy")
    nx, ny, nz = m.shape
    parts = msem.shape[0]
    step = nx // parts
    loads, stores = [], []
    for i in range(parts):
        part = pl.ds(i * step, step)
        loads.append(pltpu.make_async_copy(m_hbm.at[part], m.at[part], msem.at[i]))
        stores.append((
            pltpu.make_async_copy(nh.at[:, part], nh_hbm.at[:, part], osem.at[i]),
            pltpu.make_async_copy(ne.at[:, part], ne_hbm.at[:, part], esem.at[i]),
        ))
    for one in loads:
        one.start()

    even_x, even_y = gx % 2 == 0, gy % 2 == 0
    rows, kept = pl.ds(0, ny), pl.ds(8, ny)

    def up_z(v):
        return jnp.where(iota(v.shape, 1) == nz - 1, 0.0, pltpu.roll(v, nz - 1, 1))

    def up_row(v, edge):
        n = v.shape[0]
        return jnp.where(iota(v.shape, 0) == n - 1, edge, pltpu.roll(v, n - 1, 0))

    def either(flag, a, b):
        return jnp.where(flag, a.astype(F32), b.astype(F32))

    def rounded(v):
        return v.astype(BF16).astype(F32)

    ex, ey, ez, hx, hz = [
        either(even_y, yb_ref[pl.ds(c * nx, nx)], ya_ref[pl.ds(c * nx, nx)]) for c in range(5)
    ]
    corner = pl.ds(5 * nx, 16)
    below, above = either(even_y, yb_ref[corner], ya_ref[corner]), either(even_y, ya_ref[corner], yb_ref[corner])
    inside = jnp.where(gy > 0, 1.0, 0.0)
    low_x = rounded(inside * (2.0 * hx - ((y0_ref[1] - ez) - (up_z(ey) - ey))))
    low_z = rounded(inside * (2.0 * hz - ((up_row(ey, below[0:1]) - ey) - (y0_ref[0] - ex))))
    high[0] = either(even_y, ya_ref[pl.ds(0, nx)], yb_ref[pl.ds(0, nx)])
    high[1] = either(even_y, ya_ref[pl.ds(nx, nx)], yb_ref[pl.ds(nx, nx)])
    for x in range(nx):
        gf[0, x + 1, pl.ds(7, 1)] = low_x[x : x + 1]
        gf[2, x + 1, pl.ds(7, 1)] = low_z[x : x + 1]
    for c in range(2):
        beyond[c] = either(even_x, xa_ref[c], xb_ref[c])
    ex, ey, ez, hy, hz = [either(even_x, xb_ref[c], xa_ref[c]) for c in range(5)]
    inside = jnp.where(gx > 0, 1.0, 0.0)
    gf[1, 0, kept] = rounded(inside * (2.0 * hy - ((up_z(ex) - ex) - (ef[2, 0, rows] - ez))))
    gf[2, 0, kept] = rounded(inside * (2.0 * hz - ((ef[1, 0, rows] - ey) - (up_row(ex, above[0:1]) - ex))))

    back = 2.0 * (eye_like(0, nz) - eye_like(-1, nz))
    none = jnp.zeros((nz, nz), F32)
    wb = square(back, none, none, back)
    lane = iota((ny, nz), 1)
    table = jnp.zeros((ny, nz), F32)
    for k in range(4):
        table = jnp.where(lane == k, 0.25 * eps_ref[k], table)
    seventh = iota((8, nz), 0) == 7

    def up_y(c, which, x):
        last = jnp.where(seventh, high[which, pl.ds(x, 1)], ef[c, x, pl.ds(ny - 7, 8)])
        return jnp.concatenate([ef[c, x, pl.ds(1, ny - 8)], last], axis=0)

    def first(x):
        ey, ez = ef[1, x, rows], ef[2, x, rows]
        eyn = ef[1, x + 1, rows] if x + 1 < nx else beyond[0]
        ezn = ef[2, x + 1, rows] if x + 1 < nx else beyond[1]
        fx = hf[0, x] - (up_y(2, 1, x) - ez)
        fy = hf[1, x] + (ezn - ez)
        fz = (hf[2, x] + (up_y(0, 0, x) - ef[0, x, rows])) - (eyn - ey)
        for c, v in enumerate((fx, fy, fz)):
            g = v.astype(BF16)
            nh[c, x] = g * BF16(0.5)
            gf[c, x + 1, kept] = g.astype(F32)

    picks = lax.GatherDimensionNumbers(
        offset_dims=(), collapsed_slice_dims=(1,), start_index_map=(1,),
        operand_batching_dims=(0,), start_indices_batching_dims=(0,),
    )

    def second(x, along):
        shifted = pl.ds(7, ny)
        gx_, gy_, gz_ = [gf[c, x + 1, kept] for c in range(3)]
        coef = lax.gather(
            table, m[x][..., None], picks, (1, 1), mode=lax.GatherScatterMode.PROMISE_IN_BOUNDS
        )
        tx = (gz_ - gf[2, x + 1, shifted]) - along[:, nz:]
        ty = along[:, :nz] - (gz_ - gf[2, x, kept])
        tz = (gy_ - gf[1, x, kept]) - (gx_ - gf[0, x + 1, shifted])
        for c, t in enumerate((tx, ty, tz)):
            ne[c, x] = (ef[c, x, rows] + coef * t).astype(BF16)

    for i in range(parts + 1):
        if i > 0:
            loads[i - 1].wait()
            part = pl.ds((i - 1) * step, step)
            along = dot(side(nh[0, part], nh[1, part]), wb)
        for k in range(step):
            if i < parts:
                first(i * step + k)
            if i > 0:
                second((i - 1) * step + k, along[k * ny : (k + 1) * ny])
        if i < parts:
            stores[i][0].start()
        if i > 0:
            stores[i - 1][1].start()
    for group in stores:
        for one in group:
            one.wait()


def place_kernel(got_ref, grad_ref):
    values = jnp.transpose(got_ref[pl.ds(0, 128, stride=2), :])
    spots = got_ref[pl.ds(1, 128, stride=2), :].astype(I32)
    spots = spots[:, :4] + spots[:, 4:8]
    ranks = grad_ref.shape[1]
    total = jnp.zeros((2 * DL, ranks), F32)
    for k in range(4):
        hot = jnp.where(iota((128, ranks), 1) == spots[:, k : k + 1], 1.0, 0.0).astype(BF16)
        hi, lo = split(values[k * DL : (k + 1) * DL])
        total = total + dot(jnp.concatenate([hi, lo], axis=0), hot)
    grad_ref[...] = total[:DL] + total[DL:]


def per_device(
    adjoint_e, adjoint_h, material, inv_eps, forward_design, cell_slot, tile_pillars, pillar_rank
):
    _, nx, ny, nz = adjoint_e.shape
    sx, sy = lax.axis_size("gx"), lax.axis_size("gy")
    both = ("gx", "gy")
    shape = jax.ShapeDtypeStruct

    def stay(v):
        return pltpu.with_memory_space_constraint(v, pltpu.HBM)

    ranks = pillar_rank.reshape(512, 128)
    adjoint_e, adjoint_h, material, forward_design, cell_slot, tile_pillars, ranks = map(
        stay, (adjoint_e, adjoint_h, material, forward_design, cell_slot, tile_pillars, ranks)
    )

    def params(mib):
        return pltpu.CompilerParams(vmem_limit_bytes=mib * 1024 * 1024)

    def swap(v, axis, size, low):
        pairs = []
        for i in range(low, size - 1, 2):
            pairs += [(i, i + 1), (i + 1, i)]
        return lax.ppermute(v, axis, pairs)

    xa, xb = pl.pallas_call(
        face_kernel,
        out_shape=(shape((5, ny, nz), BF16), shape((5, ny, nz), BF16)),
        in_specs=[HBM, HBM],
        out_specs=[VM, VM],
        scratch_shapes=[pltpu.SemaphoreType.DMA((3,))],
        compiler_params=params(4),
        name="faces",
    )(adjoint_e, adjoint_h)
    xa, xb = swap(xa, "gx", sx, 0), swap(xb, "gx", sx, 1)

    send, ya, yb, y0 = pl.pallas_call(
        pillar_kernel,
        out_shape=(
            shape((256, 128), F32),
            shape((5 * nx + 16, nz), BF16), shape((5 * nx + 16, nz), BF16),
            shape((2, nx, nz), F32),
        ),
        in_specs=[HBM] * 6,
        out_specs=[VM] * 4,
        scratch_shapes=[
            pltpu.VMEM((3, nx, ny, nz), BF16), pltpu.VMEM((3, nx, ny, nz), BF16),
            pltpu.VMEM((3, nx, 8, nz), BF16), pltpu.VMEM((3, nx, 8, nz), BF16),
            pltpu.VMEM((2, nx, 8, nz), BF16),
            pltpu.VMEM((8, 512), I32), pltpu.VMEM((64, 128), I32), pltpu.VMEM((nx, ny), I32),
            pltpu.VMEM((nx, 2 * ny), I32), pltpu.VMEM((512, 128), I32),
            pltpu.VMEM((512, 2 * nz), F32),
            pltpu.SemaphoreType.DMA((PARTS,)), pltpu.SemaphoreType.DMA((PARTS,)),
            pltpu.SemaphoreType.DMA((7,)),
        ],
        compiler_params=params(12),
        name="pillars",
    )(adjoint_e, adjoint_h, forward_design, cell_slot, tile_pillars, ranks)

    got = lax.all_to_all(send.reshape(128, 2, 128), both, 0, 0, tiled=True)
    got = got.reshape(256, 128)

    even_x, even_y = lax.axis_index("gx") % 2 == 0, lax.axis_index("gy") % 2 == 0
    up = jnp.where(even_x, xa[0, ny - 1 :], xb[0, ny - 1 :])
    down = jnp.where(even_x, xb[0, :1], xa[0, :1])
    ya = lax.dynamic_update_slice(ya, jnp.where(even_y, up, down), (5 * nx, 0))
    yb = lax.dynamic_update_slice(yb, jnp.where(even_y, down, up), (5 * nx, 0))
    ya = swap(ya, "gy", sy, 0)
    yb = swap(yb, "gy", sy, 1)

    ef, hf = pl.pallas_call(
        spread_kernel,
        out_shape=(shape((3, nx, ny + 8, nz), F32), shape((3, nx, ny, nz), F32)),
        in_specs=[HBM, HBM],
        out_specs=[VM, VM],
        scratch_shapes=[
            pltpu.VMEM((3, nx, ny, nz), BF16), pltpu.VMEM((3, nx, ny, nz), BF16),
            pltpu.SemaphoreType.DMA((PARTS,)), pltpu.SemaphoreType.DMA((PARTS,)),
        ],
        compiler_params=params(16),
        name="spread",
    )(adjoint_e, adjoint_h)

    new_e, new_h = pl.pallas_call(
        field_kernel,
        out_shape=(shape(adjoint_e.shape, BF16), shape(adjoint_e.shape, BF16)),
        in_specs=[VM, VM, HBM, SM] + [VM] * 5,
        out_specs=[HBM, HBM],
        scratch_shapes=[
            pltpu.VMEM((nx, ny, nz), I32),
            pltpu.VMEM((3, nx, ny, nz), BF16), pltpu.VMEM((3, nx, ny, nz), BF16),
            pltpu.VMEM((3, nx + 1, ny + 8, nz), F32),
            pltpu.VMEM((2, nx, nz), F32), pltpu.VMEM((2, ny, nz), F32),
        ] + [pltpu.SemaphoreType.DMA((CHUNKS,))] * 3,
        compiler_params=params(20),
        name="fields",
    )(ef, hf, material, inv_eps, xa, xb, ya, yb, y0)

    gradient = pl.pallas_call(
        place_kernel,
        out_shape=shape((DL, 512), F32),
        in_specs=[VM],
        out_specs=VM,
        compiler_params=params(4),
        name="place",
    )(got)
    return new_e, new_h, gradient


def solution(mesh):
    return jax.shard_map(
        per_device,
        mesh=mesh,
        in_specs=(
            P(None, "gx", "gy", None),
            P(None, "gx", "gy", None),
            P("gx", "gy", None),
            P(),
            P(None, "gx", "gy", None),
            P("gx", "gy"),
            P(),
            P(),
        ),
        out_specs=(P(None, "gx", "gy", None), P(None, "gx", "gy", None), P(None, ("gx", "gy"))),
        check_vma=False,
    )
```

```python
import jax
import jax.numpy as jnp
from jax import lax
from jax.experimental import pallas as pl
from jax.experimental.pallas import tpu as pltpu
from jax.sharding import PartitionSpec as P

F32, BF16, I32 = jnp.float32, jnp.bfloat16, jnp.int32
HBM = pl.BlockSpec(memory_space=pltpu.HBM)
VM = pl.BlockSpec(memory_space=pltpu.VMEM)
SM = pl.BlockSpec(memory_space=pltpu.SMEM)
DL = 32
CHUNKS = 8
PARTS = 4


def split(v):
    hi = v.astype(BF16)
    return hi, (v - hi.astype(F32)).astype(BF16)


def iota(shape, axis):
    return lax.broadcasted_iota(I32, shape, axis)


def dot(a, b):
    return jnp.dot(a, b, preferred_element_type=F32)


def face_kernel(e_hbm, h_hbm, a_ref, b_ref, sem):
    gx = lax.axis_index("gx")
    last = e_hbm.shape[1] - 1

    def fill(up_ref, down_ref):
        copies = [
            pltpu.make_async_copy(e_hbm.at[:, last], up_ref.at[pl.ds(0, 3)], sem.at[0]),
            pltpu.make_async_copy(h_hbm.at[pl.ds(1, 2), last], up_ref.at[pl.ds(3, 2)], sem.at[1]),
            pltpu.make_async_copy(e_hbm.at[pl.ds(1, 2), 0], down_ref.at[pl.ds(0, 2)], sem.at[2]),
        ]
        for one in copies:
            one.start()
        down_ref[pl.ds(2, 3)] = jnp.zeros((3,) + down_ref.shape[1:], BF16)
        for one in copies:
            one.wait()

    @pl.when(gx % 2 == 0)
    def _():
        fill(a_ref, b_ref)

    @pl.when(gx % 2 == 1)
    def _():
        fill(b_ref, a_ref)


def lookup(table, index):
    rows = index.shape[0]
    result = jnp.zeros(index.shape, table.dtype)
    for q in range(4):
        part = jnp.broadcast_to(table[q : q + 1], (rows, 128))
        taken = jnp.take_along_axis(part, index & 127, axis=1, mode="promise_in_bounds")
        result = jnp.where(index >> 7 == q, taken, result)
    return result


def pillar_kernel(
    e_hbm, h_hbm, m_hbm, f_hbm, slot_hbm, tiles_hbm, rank_hbm,
    send_ref, ya_ref, yb_ref, y0_ref, e, m,
    f, y_first, y_last, y_h, tiles, rank, slot, cells, ids, acc, sem, fsem, msem,
):
    gx, gy = lax.axis_index("gx"), lax.axis_index("gy")
    _, nx, ny, nz = e.shape
    parts = sem.shape[0]
    step = nx // parts
    copies = []
    for i in range(parts):
        part = pl.ds(i * step, step)
        copies.append((
            pltpu.make_async_copy(e_hbm.at[:, part], e.at[:, part], sem.at[i]),
            pltpu.make_async_copy(f_hbm.at[:, part], f.at[:, part], fsem.at[i]),
        ))
    extra = [
        pltpu.make_async_copy(tiles_hbm.at[gx, pl.ds(gy // 8 * 8, 8)], tiles, msem.at[0]),
        pltpu.make_async_copy(rank_hbm.at[pl.ds(gx * 64, 64)], rank, msem.at[1]),
        pltpu.make_async_copy(slot_hbm, slot, msem.at[2]),
        pltpu.make_async_copy(e_hbm.at[:, :, pl.ds(0, 8)], y_first, msem.at[3]),
        pltpu.make_async_copy(e_hbm.at[:, :, pl.ds(ny - 8, 8)], y_last, msem.at[4]),
        pltpu.make_async_copy(h_hbm.at[0, :, pl.ds(ny - 8, 8)], y_h.at[0], msem.at[5]),
        pltpu.make_async_copy(h_hbm.at[2, :, pl.ds(ny - 8, 8)], y_h.at[1], msem.at[6]),
        pltpu.make_async_copy(m_hbm, m, msem.at[7]),
    ]
    for one in extra[:3]:
        one.start()
    for one, two in copies[:1]:
        one.start()
        two.start()
    for one, two in copies[1:]:
        one.start()
        two.start()
    for one in extra[3:]:
        one.start()
    ids[...] = iota(ids.shape, 0)
    lanes, rows = iota((128, 128), 1), iota((128, 128), 0)

    for one in extra[:3]:
        one.wait()
    quarter = gy // 4
    ranks = rank[pl.ds(0, 16, stride=4), :]
    for q in range(1, 4):
        ranks = jnp.where(quarter == q, rank[pl.ds(q, 16, stride=4), :], ranks)
    turned = ranks
    for q in range(1, 4):
        turned = jnp.where(gy % 4 == q, pltpu.roll(ranks, 128 - 32 * q, 1), turned)
    moved = [turned] + [pltpu.roll(turned, 32 * q, 1) for q in range(1, 4)]
    lane = iota((1, 128), 1)
    own_rank = []
    for q in range(4):
        line = moved[0][4 * q : 4 * q + 1]
        for k in range(1, 4):
            line = jnp.where(lane >> 5 == k, moved[k][4 * q + k : 4 * q + k + 1], line)
        own_rank.append(line)
    owner = [line >> 9 for line in own_rank]
    hits = [rows == line for line in owner]
    ones = [jnp.where(hit, 1.0, 0.0).astype(BF16) for hit in hits]
    counter = jnp.concatenate(
        [jnp.where(rows < lanes, 1.0, 0.0), jnp.ones((128, 128), F32)], axis=1
    ).astype(BF16)
    before = jnp.zeros((128, 128), F32)
    turn = []
    for q in range(4):
        both = dot(ones[q], counter)
        count = both[:, :128] + before
        turn.append(jnp.sum(jnp.where(hits[q], count, 0.0), axis=0, keepdims=True).astype(I32))
        before = before + both[:, 128:]
    spots = []
    for q in range(4):
        place = own_rank[q] & 511
        eight = jnp.where(iota((16, 128), 0) < 4, place & 255, place & 256)
        mine = (iota((16, 128), 0) & 3 == turn[q]) & (iota((16, 128), 0) < 8)
        spots.append(jnp.where(mine, eight, 0).astype(F32).astype(BF16))
    spots = lax.dot_general(
        jnp.concatenate(ones, axis=1), jnp.concatenate(spots, axis=1),
        (((1,), (1,)), ((), ())), preferred_element_type=F32,
    )
    send_ref[pl.ds(1, 128, stride=2), :] = jnp.concatenate([spots, jnp.zeros((128, 112), F32)], axis=1)
    target = jnp.concatenate([turn[q] * 128 + owner[q] for q in range(4)], axis=0)
    own = jnp.sum(jnp.where(iota(tiles.shape, 0) == gy % 8, tiles[...], 0), axis=0, keepdims=True)
    own = jnp.concatenate([own[:, 128 * q : 128 * (q + 1)] for q in range(4)], axis=0)
    canon = ((own >> 9) & 15) * 32 + (own & 31)
    target = lookup(target, canon)
    cells[:, :ny] = slot[...]
    cells[:, ny:] = slot[...]
    half = nx // 2
    pair = jnp.where(
        iota((half, 2 * ny), 1) < ny,
        cells[pl.ds(0, half, stride=2), :], cells[pl.ds(1, half, stride=2), :],
    )
    pair = lookup(target, pair)

    for i, (one, two) in enumerate(copies):
        one.wait()
        two.wait()
        part = pl.ds(i * step, step)
        density = e[0, part].astype(F32) * f[0, part].astype(F32)
        for c in range(1, 3):
            density = density + e[c, part].astype(F32) * f[c, part].astype(F32)
        both = jnp.concatenate(split(density.reshape(step * ny, nz)), axis=1)
        hot = jnp.concatenate(
            [
                jnp.where(ids[...] == pair[p : p + 1], 1.0, 0.0).astype(BF16)
                for p in range(i * step // 2, (i + 1) * step // 2)
            ],
            axis=1,
        )
        total = dot(hot, both)
        if i == 0:
            acc[...] = total
        elif i + 1 < parts:
            acc[...] += total
    total = acc[...] + total
    values = jnp.zeros((128, 128), F32)
    for k in range(4):
        part = total[k * 128 : (k + 1) * 128]
        hi, lo = split(part[:, :nz] + part[:, nz:])
        gather = jnp.where(lanes == 32 * k + (rows >> 2), 0.125, 0.0).astype(BF16)
        values = values + dot(hi, gather) + dot(lo, gather)
    send_ref[pl.ds(0, 128, stride=2), :] = values

    for one in extra[3:7]:
        one.wait()
    at = iota((nx, 8 * nx), 1) - 8 * iota((nx, 8 * nx), 0)
    low = jnp.where(at == 0, 1.0, 0.0).astype(BF16)
    high = jnp.where(at == 7, 1.0, 0.0).astype(BF16)

    def face(which, one, two):
        both = jnp.concatenate([one.reshape(8 * nx, nz), two.reshape(8 * nx, nz)], axis=1)
        both = dot(which, both)
        return both[:, :nz], both[:, nz:]

    y0x, y0z = face(low, y_first[0], y_first[2])
    up_y = face(high, y_last[0], y_last[1]) + face(high, y_last[2], y_h[0]) + face(high, y_h[1], y_h[1])[:1]
    y0_ref[0] = y0x
    y0_ref[1] = y0z

    def pack(up_ref, down_ref):
        for c in range(5):
            up_ref[pl.ds(c * nx, nx)] = up_y[c].astype(BF16)
        down_ref[pl.ds(0, nx)] = y0x.astype(BF16)
        down_ref[pl.ds(nx, nx)] = y0z.astype(BF16)
        down_ref[pl.ds(2 * nx, 3 * nx)] = jnp.zeros((3 * nx, nz), BF16)
        up_ref[pl.ds(5 * nx, 16)] = jnp.zeros((16, nz), BF16)
        down_ref[pl.ds(5 * nx, 16)] = jnp.zeros((16, nz), BF16)

    @pl.when(gy % 2 == 0)
    def _():
        pack(ya_ref, yb_ref)

    @pl.when(gy % 2 == 1)
    def _():
        pack(yb_ref, ya_ref)

    for one in extra[7:]:
        one.wait()


def eye_like(distance, n):
    return jnp.where(iota((n, n), 0) == iota((n, n), 1) + distance, 1.0, 0.0)


def square(a, b, c, d):
    top, bottom = jnp.concatenate([a, b], axis=1), jnp.concatenate([c, d], axis=1)
    return jnp.concatenate([top, bottom], axis=0).astype(BF16)


def side(one, two):
    shape = (one.shape[0] * one.shape[1], one.shape[2])
    return jnp.concatenate([one.reshape(shape), two.reshape(shape)], axis=1)


def spread_kernel(e, h_hbm, m, eps_ref, ef_ref, hf_ref, cf_ref, h, sem):
    nx, ny, nz = m.shape
    step = nx // PARTS
    loads = []
    for i in range(PARTS):
        part = pl.ds(i * step, step)
        loads.append(pltpu.make_async_copy(h_hbm.at[:, part], h.at[:, part], sem.at[i]))
    for one in loads:
        one.start()
    values = [0.25 * eps_ref[k] for k in range(4)]
    eye = eye_like(0, nz)
    ahead = eye_like(1, nz) - eye
    none = jnp.zeros((nz, nz), F32)
    wx = square(2.0 * eye, none, ahead, eye)
    wy = square(2.0 * eye, none, -ahead, eye)
    for x in range(nx):
        kind = m[x]
        cf_ref[x] = jnp.where(
            kind < 2, jnp.where(kind == 0, values[0], values[1]), jnp.where(kind == 2, values[2], values[3])
        )
        ef_ref[2, x, pl.ds(0, ny)] = e[2, x].astype(F32)
    for i in range(PARTS):
        loads[i].wait()
        part = pl.ds(i * step, step)
        for c, other, w in ((0, 1, wx), (1, 0, wy)):
            both = dot(side(h[c, part], e[other, part]), w)
            for k in range(step):
                x = i * step + k
                line = both[k * ny : (k + 1) * ny]
                hf_ref[c, x] = line[:, :nz]
                ef_ref[other, x, pl.ds(0, ny)] = line[:, nz:]
        for k in range(step):
            x = i * step + k
            hz = h[2, x].astype(F32)
            hf_ref[2, x] = hz + hz


def field_kernel(
    ef, hf, cf, xa_ref, xb_ref, ya_ref, yb_ref, y0_ref,
    ne_hbm, nh_hbm,
    ne, nh, gf, bz, high, beyond, esem, osem,
):
    gx, gy = lax.axis_index("gx"), lax.axis_index("gy")
    nx, ny, nz = cf.shape
    parts = esem.shape[0]
    step = nx // parts
    stores = []
    for i in range(parts):
        part = pl.ds(i * step, step)
        stores.append((
            pltpu.make_async_copy(nh.at[:, part], nh_hbm.at[:, part], osem.at[i]),
            pltpu.make_async_copy(ne.at[:, part], ne_hbm.at[:, part], esem.at[i]),
        ))

    even_x, even_y = gx % 2 == 0, gy % 2 == 0
    rows, kept = pl.ds(0, ny), pl.ds(8, ny)

    def up_z(v):
        return jnp.where(iota(v.shape, 1) == nz - 1, 0.0, pltpu.roll(v, nz - 1, 1))

    def up_row(v, edge):
        n = v.shape[0]
        return jnp.where(iota(v.shape, 0) == n - 1, edge, pltpu.roll(v, n - 1, 0))

    def either(flag, a, b):
        return jnp.where(flag, a.astype(F32), b.astype(F32))

    def rounded(v):
        return v.astype(BF16).astype(F32)

    ex, ey, ez, hx, hz = [
        either(even_y, yb_ref[pl.ds(c * nx, nx)], ya_ref[pl.ds(c * nx, nx)]) for c in range(5)
    ]
    corner = pl.ds(5 * nx, 16)
    below, above = either(even_y, yb_ref[corner], ya_ref[corner]), either(even_y, ya_ref[corner], yb_ref[corner])
    inside = jnp.where(gy > 0, 1.0, 0.0)
    low_x = rounded(inside * (2.0 * hx - ((y0_ref[1] - ez) - (up_z(ey) - ey))))
    low_z = rounded(inside * (2.0 * hz - ((up_row(ey, below[0:1]) - ey) - (y0_ref[0] - ex))))
    high[0] = either(even_y, ya_ref[pl.ds(0, nx)], yb_ref[pl.ds(0, nx)])
    high[1] = either(even_y, ya_ref[pl.ds(nx, nx)], yb_ref[pl.ds(nx, nx)])
    for x in range(nx):
        gf[0, x + 1, pl.ds(7, 1)] = low_x[x : x + 1]
        gf[2, x + 1, pl.ds(7, 1)] = low_z[x : x + 1]
    for c in range(2):
        beyond[c] = either(even_x, xa_ref[c], xb_ref[c])
    ex, ey, ez, hy, hz = [either(even_x, xb_ref[c], xa_ref[c]) for c in range(5)]
    inside = jnp.where(gx > 0, 1.0, 0.0)
    gf[1, 0, kept] = rounded(inside * (2.0 * hy - ((up_z(ex) - ex) - (ef[2, 0, rows] - ez))))
    gf[2, 0, kept] = rounded(inside * (2.0 * hz - ((ef[1, 0, rows] - ey) - (up_row(ex, above[0:1]) - ex))))

    back = 2.0 * (eye_like(0, nz) - eye_like(-1, nz))
    none = jnp.zeros((nz, nz), F32)
    wb = square(back, none, none, back)
    seventh = iota((8, nz), 0) == 7

    def up_y(c, which, x):
        last = jnp.where(seventh, high[which, pl.ds(x, 1)], ef[c, x, pl.ds(ny - 7, 8)])
        return jnp.concatenate([ef[c, x, pl.ds(1, ny - 8)], last], axis=0)

    def first(x):
        ey, ez = ef[1, x, rows], ef[2, x, rows]
        eyn = ef[1, x + 1, rows] if x + 1 < nx else beyond[0]
        ezn = ef[2, x + 1, rows] if x + 1 < nx else beyond[1]
        fx = hf[0, x] - (up_y(2, 1, x) - ez)
        fy = hf[1, x] + (ezn - ez)
        fz = (hf[2, x] + (up_y(0, 0, x) - ef[0, x, rows])) - (eyn - ey)
        for c, v in enumerate((fx, fy, fz)):
            g = v.astype(BF16)
            nh[c, x] = g * BF16(0.5)
            gf[c, x + 1, kept] = g.astype(F32)

    def second(x):
        shifted = pl.ds(7, ny)
        gx_, gy_, gz_ = [gf[c, x + 1, kept] for c in range(3)]
        slot = pl.ds(x % (2 * step) * ny, ny)
        tx = (gz_ - gf[2, x + 1, shifted]) - bz[1, slot]
        ty = bz[0, slot] - (gz_ - gf[2, x, kept])
        tz = (gy_ - gf[1, x, kept]) - (gx_ - gf[0, x + 1, shifted])
        coef = cf[x]
        for c, t in enumerate((tx, ty, tz)):
            ne[c, x] = (ef[c, x, rows] + coef * t).astype(BF16)

    for i in range(parts + 1):
        for k in range(step):
            if i < parts:
                first(i * step + k)
        if i < parts:
            part = pl.ds(i * step, step)
            both = dot(side(nh[0, part], nh[1, part]), wb)
            slot = pl.ds(i % 2 * step * ny, step * ny)
            bz[0, slot] = both[:, :nz]
            bz[1, slot] = both[:, nz:]
        for k in range(step):
            if i > 0:
                second((i - 1) * step + k)
        if i < parts:
            stores[i][0].start()
        if i > 0:
            stores[i - 1][1].start()
    for group in stores:
        for one in group:
            one.wait()


def place_kernel(got_ref, grad_ref):
    values = jnp.transpose(got_ref[pl.ds(0, 128, stride=2), :])
    spots = got_ref[pl.ds(1, 128, stride=2), :].astype(I32)
    spots = spots[:, :4] + spots[:, 4:8]
    ranks = grad_ref.shape[1]
    total = jnp.zeros((2 * DL, ranks), F32)
    for k in range(4):
        hot = jnp.where(iota((128, ranks), 1) == spots[:, k : k + 1], 1.0, 0.0).astype(BF16)
        hi, lo = split(values[k * DL : (k + 1) * DL])
        total = total + dot(jnp.concatenate([hi, lo], axis=0), hot)
    grad_ref[...] = total[:DL] + total[DL:]


def per_device(
    adjoint_e, adjoint_h, material, inv_eps, forward_design, cell_slot, tile_pillars, pillar_rank
):
    _, nx, ny, nz = adjoint_e.shape
    sx, sy = lax.axis_size("gx"), lax.axis_size("gy")
    both = ("gx", "gy")
    shape = jax.ShapeDtypeStruct

    def stay(v):
        return pltpu.with_memory_space_constraint(v, pltpu.HBM)

    ranks = pillar_rank.reshape(512, 128)
    adjoint_e, adjoint_h, material, forward_design, cell_slot, tile_pillars, ranks = map(
        stay, (adjoint_e, adjoint_h, material, forward_design, cell_slot, tile_pillars, ranks)
    )

    def params(mib):
        return pltpu.CompilerParams(vmem_limit_bytes=mib * 1024 * 1024)

    def swap(v, axis, size, low):
        pairs = []
        for i in range(low, size - 1, 2):
            pairs += [(i, i + 1), (i + 1, i)]
        return lax.ppermute(v, axis, pairs)

    xa, xb = pl.pallas_call(
        face_kernel,
        out_shape=(shape((5, ny, nz), BF16), shape((5, ny, nz), BF16)),
        in_specs=[HBM, HBM],
        out_specs=[VM, VM],
        scratch_shapes=[pltpu.SemaphoreType.DMA((3,))],
        compiler_params=params(4),
        name="faces",
    )(adjoint_e, adjoint_h)
    xa, xb = swap(xa, "gx", sx, 0), swap(xb, "gx", sx, 1)

    send, ya, yb, y0, e_vm, m_vm = pl.pallas_call(
        pillar_kernel,
        out_shape=(
            shape((256, 128), F32),
            shape((5 * nx + 16, nz), BF16), shape((5 * nx + 16, nz), BF16),
            shape((2, nx, nz), F32),
            shape(adjoint_e.shape, BF16), shape((nx, ny, nz), I32),
        ),
        in_specs=[HBM] * 7,
        out_specs=[VM] * 6,
        scratch_shapes=[
            pltpu.VMEM((3, nx, ny, nz), BF16),
            pltpu.VMEM((3, nx, 8, nz), BF16), pltpu.VMEM((3, nx, 8, nz), BF16),
            pltpu.VMEM((2, nx, 8, nz), BF16),
            pltpu.VMEM((8, 512), I32), pltpu.VMEM((64, 128), I32), pltpu.VMEM((nx, ny), I32),
            pltpu.VMEM((nx, 2 * ny), I32), pltpu.VMEM((512, 128), I32),
            pltpu.VMEM((512, 2 * nz), F32),
            pltpu.SemaphoreType.DMA((PARTS,)), pltpu.SemaphoreType.DMA((PARTS,)),
            pltpu.SemaphoreType.DMA((8,)),
        ],
        compiler_params=params(12),
        name="pillars",
    )(adjoint_e, adjoint_h, material, forward_design, cell_slot, tile_pillars, ranks)

    got = lax.all_to_all(send.reshape(128, 2, 128), both, 0, 0, tiled=True)
    got = got.reshape(256, 128)

    even_x, even_y = lax.axis_index("gx") % 2 == 0, lax.axis_index("gy") % 2 == 0
    up = jnp.where(even_x, xa[0, ny - 1 :], xb[0, ny - 1 :])
    down = jnp.where(even_x, xb[0, :1], xa[0, :1])
    ya = lax.dynamic_update_slice(ya, jnp.where(even_y, up, down), (5 * nx, 0))
    yb = lax.dynamic_update_slice(yb, jnp.where(even_y, down, up), (5 * nx, 0))
    ya = swap(ya, "gy", sy, 0)
    yb = swap(yb, "gy", sy, 1)

    ef, hf, cf = pl.pallas_call(
        spread_kernel,
        out_shape=(
            shape((3, nx, ny + 8, nz), F32), shape((3, nx, ny, nz), F32), shape((nx, ny, nz), F32)
        ),
        in_specs=[VM, HBM, VM, SM],
        out_specs=[VM] * 3,
        scratch_shapes=[pltpu.VMEM((3, nx, ny, nz), BF16), pltpu.SemaphoreType.DMA((PARTS,))],
        compiler_params=params(16),
        name="spread",
    )(e_vm, adjoint_h, m_vm, inv_eps)

    new_e, new_h = pl.pallas_call(
        field_kernel,
        out_shape=(shape(adjoint_e.shape, BF16), shape(adjoint_e.shape, BF16)),
        in_specs=[VM] * 8,
        out_specs=[HBM, HBM],
        scratch_shapes=[
            pltpu.VMEM((3, nx, ny, nz), BF16), pltpu.VMEM((3, nx, ny, nz), BF16),
            pltpu.VMEM((3, nx + 1, ny + 8, nz), F32),
            pltpu.VMEM((2, 2 * nx // CHUNKS * ny, nz), F32),
            pltpu.VMEM((2, nx, nz), F32), pltpu.VMEM((2, ny, nz), F32),
        ] + [pltpu.SemaphoreType.DMA((CHUNKS,))] * 2,
        compiler_params=params(20),
        name="fields",
    )(ef, hf, cf, xa, xb, ya, yb, y0)

    gradient = pl.pallas_call(
        place_kernel,
        out_shape=shape((DL, 512), F32),
        in_specs=[VM],
        out_specs=VM,
        compiler_params=params(4),
        name="place",
    )(got)
    return new_e, new_h, gradient


def solution(mesh):
    return jax.shard_map(
        per_device,
        mesh=mesh,
        in_specs=(
            P(None, "gx", "gy", None),
            P(None, "gx", "gy", None),
            P("gx", "gy", None),
            P(),
            P(None, "gx", "gy", None),
            P("gx", "gy"),
            P(),
            P(),
        ),
        out_specs=(P(None, "gx", "gy", None), P(None, "gx", "gy", None), P(None, ("gx", "gy"))),
        check_vma=False,
    )
```

```python
import jax
import jax.numpy as jnp
from jax import lax
from jax.experimental import pallas as pl
from jax.experimental.pallas import tpu as pltpu
from jax.sharding import PartitionSpec as P

F32, BF16, I32 = jnp.float32, jnp.bfloat16, jnp.int32
HBM = pl.BlockSpec(memory_space=pltpu.HBM)
VM = pl.BlockSpec(memory_space=pltpu.VMEM)
SM = pl.BlockSpec(memory_space=pltpu.SMEM)
DL = 32
CHUNKS = 8
PARTS = 4


def split(v):
    hi = v.astype(BF16)
    return hi, (v - hi.astype(F32)).astype(BF16)


def iota(shape, axis):
    return lax.broadcasted_iota(I32, shape, axis)


def dot(a, b):
    return jnp.dot(a, b, preferred_element_type=F32)


def lookup(table, index):
    rows = index.shape[0]
    result = jnp.zeros(index.shape, table.dtype)
    for q in range(4):
        part = jnp.broadcast_to(table[q : q + 1], (rows, 128))
        taken = jnp.take_along_axis(part, index & 127, axis=1, mode="promise_in_bounds")
        result = jnp.where(index >> 7 == q, taken, result)
    return result


def pillar_kernel(
    e_hbm, h_hbm, m_hbm, f_hbm, slot_hbm, tiles_hbm, rank_hbm,
    sent_ref, xa_ref, xb_ref, ya_ref, yb_ref, y0_ref, e, m,
    send_ref, f, y_first, y_last, y_h, tiles, rank, slot, cells, ids, acc, sem, fsem, msem, xsem,
):
    gx, gy = lax.axis_index("gx"), lax.axis_index("gy")
    _, nx, ny, nz = e.shape
    parts = sem.shape[0]
    step = nx // parts
    copies = []
    for i in range(parts):
        part = pl.ds(i * step, step)
        copies.append((
            pltpu.make_async_copy(e_hbm.at[:, part], e.at[:, part], sem.at[i]),
            pltpu.make_async_copy(f_hbm.at[:, part], f.at[:, part], fsem.at[i]),
        ))
    extra = [
        pltpu.make_async_copy(tiles_hbm.at[gx, pl.ds(gy // 8 * 8, 8)], tiles, msem.at[0]),
        pltpu.make_async_copy(rank_hbm.at[pl.ds(gx * 64, 64)], rank, msem.at[1]),
        pltpu.make_async_copy(slot_hbm, slot, msem.at[2]),
        pltpu.make_async_copy(e_hbm.at[:, :, pl.ds(0, 8)], y_first, msem.at[3]),
        pltpu.make_async_copy(e_hbm.at[:, :, pl.ds(ny - 8, 8)], y_last, msem.at[4]),
        pltpu.make_async_copy(h_hbm.at[0, :, pl.ds(ny - 8, 8)], y_h.at[0], msem.at[5]),
        pltpu.make_async_copy(h_hbm.at[2, :, pl.ds(ny - 8, 8)], y_h.at[1], msem.at[6]),
        pltpu.make_async_copy(m_hbm, m, msem.at[7]),
    ]
    for one in extra[:3]:
        one.start()
    for one, two in copies[:1]:
        one.start()
        two.start()
    for one, two in copies[1:]:
        one.start()
        two.start()
    for one in extra[3:]:
        one.start()

    def faces(up_ref, down_ref):
        return [
            pltpu.make_async_copy(e_hbm.at[:, nx - 1], up_ref.at[pl.ds(0, 3)], xsem.at[0]),
            pltpu.make_async_copy(h_hbm.at[pl.ds(1, 2), nx - 1], up_ref.at[pl.ds(3, 2)], xsem.at[1]),
            pltpu.make_async_copy(e_hbm.at[pl.ds(1, 2), 0], down_ref.at[pl.ds(0, 2)], xsem.at[2]),
        ]

    @pl.when(gx % 2 == 0)
    def _():
        for one in faces(xa_ref, xb_ref):
            one.start()
        xb_ref[pl.ds(2, 3)] = jnp.zeros((3, ny, nz), BF16)

    @pl.when(gx % 2 == 1)
    def _():
        for one in faces(xb_ref, xa_ref):
            one.start()
        xa_ref[pl.ds(2, 3)] = jnp.zeros((3, ny, nz), BF16)

    ids[...] = iota(ids.shape, 0)
    lanes, rows = iota((128, 128), 1), iota((128, 128), 0)

    for one in extra[:3]:
        one.wait()
    quarter = gy // 4
    ranks = rank[pl.ds(0, 16, stride=4), :]
    for q in range(1, 4):
        ranks = jnp.where(quarter == q, rank[pl.ds(q, 16, stride=4), :], ranks)
    turned = ranks
    for q in range(1, 4):
        turned = jnp.where(gy % 4 == q, pltpu.roll(ranks, 128 - 32 * q, 1), turned)
    moved = [turned] + [pltpu.roll(turned, 32 * q, 1) for q in range(1, 4)]
    lane = iota((1, 128), 1)
    own_rank = []
    for q in range(4):
        line = moved[0][4 * q : 4 * q + 1]
        for k in range(1, 4):
            line = jnp.where(lane >> 5 == k, moved[k][4 * q + k : 4 * q + k + 1], line)
        own_rank.append(line)
    owner = [line >> 9 for line in own_rank]
    hits = [rows == line for line in owner]
    ones = [jnp.where(hit, 1.0, 0.0).astype(BF16) for hit in hits]
    counter = jnp.concatenate(
        [jnp.where(rows < lanes, 1.0, 0.0), jnp.ones((128, 128), F32)], axis=1
    ).astype(BF16)
    before = jnp.zeros((128, 128), F32)
    turn = []
    for q in range(4):
        both = dot(ones[q], counter)
        count = both[:, :128] + before
        turn.append(jnp.sum(jnp.where(hits[q], count, 0.0), axis=0, keepdims=True).astype(I32))
        before = before + both[:, 128:]
    spots = []
    for q in range(4):
        place = own_rank[q] & 511
        eight = jnp.where(iota((16, 128), 0) < 4, place & 255, place & 256)
        mine = (iota((16, 128), 0) & 3 == turn[q]) & (iota((16, 128), 0) < 8)
        spots.append(jnp.where(mine, eight, 0).astype(F32).astype(BF16))
    spots = lax.dot_general(
        jnp.concatenate(ones, axis=1), jnp.concatenate(spots, axis=1),
        (((1,), (1,)), ((), ())), preferred_element_type=F32,
    )
    send_ref[pl.ds(2, 128, stride=4), :] = jnp.concatenate([spots, jnp.zeros((128, 112), F32)], axis=1)
    target = jnp.concatenate([turn[q] * 128 + owner[q] for q in range(4)], axis=0)
    own = jnp.sum(jnp.where(iota(tiles.shape, 0) == gy % 8, tiles[...], 0), axis=0, keepdims=True)
    own = jnp.concatenate([own[:, 128 * q : 128 * (q + 1)] for q in range(4)], axis=0)
    canon = ((own >> 9) & 15) * 32 + (own & 31)
    target = lookup(target, canon)
    cells[:, :ny] = slot[...]
    cells[:, ny:] = slot[...]
    half = nx // 2
    pair = jnp.where(
        iota((half, 2 * ny), 1) < ny,
        cells[pl.ds(0, half, stride=2), :], cells[pl.ds(1, half, stride=2), :],
    )
    pair = lookup(target, pair)

    for i, (one, two) in enumerate(copies):
        one.wait()
        two.wait()
        part = pl.ds(i * step, step)
        density = e[0, part].astype(F32) * f[0, part].astype(F32)
        for c in range(1, 3):
            density = density + e[c, part].astype(F32) * f[c, part].astype(F32)
        both = jnp.concatenate(split(density.reshape(step * ny, nz)), axis=1)
        hot = jnp.concatenate(
            [
                jnp.where(ids[...] == pair[p : p + 1], 1.0, 0.0).astype(BF16)
                for p in range(i * step // 2, (i + 1) * step // 2)
            ],
            axis=1,
        )
        total = dot(hot, both)
        if i == 0:
            acc[...] = total
        elif i + 1 < parts:
            acc[...] += total
    total = acc[...] + total
    values = jnp.zeros((128, 128), F32)
    for k in range(4):
        part = total[k * 128 : (k + 1) * 128]
        hi, lo = split(part[:, :nz] + part[:, nz:])
        gather = jnp.where(lanes == 32 * k + (rows >> 2), 0.125, 0.0).astype(BF16)
        values = values + dot(hi, gather) + dot(lo, gather)
    hi, lo = split(values)
    send_ref[pl.ds(0, 128, stride=4), :] = hi.astype(F32)
    send_ref[pl.ds(1, 128, stride=4), :] = lo.astype(F32)

    for one in extra[3:7]:
        one.wait()
    at = iota((nx, 8 * nx), 1) - 8 * iota((nx, 8 * nx), 0)
    low = jnp.where(at == 0, 1.0, 0.0).astype(BF16)
    high = jnp.where(at == 7, 1.0, 0.0).astype(BF16)

    def face(which, one, two):
        both = jnp.concatenate([one.reshape(8 * nx, nz), two.reshape(8 * nx, nz)], axis=1)
        both = dot(which, both)
        return both[:, :nz], both[:, nz:]

    y0x, y0z = face(low, y_first[0], y_first[2])
    up_y = face(high, y_last[0], y_last[1]) + face(high, y_last[2], y_h[0]) + face(high, y_h[1], y_h[1])[:1]
    y0_ref[0] = y0x
    y0_ref[1] = y0z

    sx, sy = lax.axis_size("gx"), lax.axis_size("gy")
    send_ref[pl.ds(3, 128, stride=4), :] = jnp.zeros((128, nz), F32)

    @pl.when((gx < sx - 1) & (gy > 0))
    def _():
        send_ref[pl.ds(4 * ((gx + 1) * sy + gy - 1) + 3, 1), :] = y0x[nx - 1 :]

    @pl.when((gx > 0) & (gy < sy - 1))
    def _():
        send_ref[pl.ds(4 * ((gx - 1) * sy + gy + 1) + 3, 1), :] = up_y[1][:1]

    sent_ref[...] = send_ref[...].astype(BF16)

    def pack(up_ref, down_ref):
        for c in range(5):
            up_ref[pl.ds(c * nx, nx)] = up_y[c].astype(BF16)
        down_ref[pl.ds(0, nx)] = y0x.astype(BF16)
        down_ref[pl.ds(nx, nx)] = y0z.astype(BF16)
        down_ref[pl.ds(2 * nx, 3 * nx)] = jnp.zeros((3 * nx, nz), BF16)

    @pl.when(gy % 2 == 0)
    def _():
        pack(ya_ref, yb_ref)

    @pl.when(gy % 2 == 1)
    def _():
        pack(yb_ref, ya_ref)

    for one in extra[7:] + faces(xa_ref, xb_ref):
        one.wait()


def eye_like(distance, n):
    return jnp.where(iota((n, n), 0) == iota((n, n), 1) + distance, 1.0, 0.0)


def square(a, b, c, d):
    top, bottom = jnp.concatenate([a, b], axis=1), jnp.concatenate([c, d], axis=1)
    return jnp.concatenate([top, bottom], axis=0).astype(BF16)


def side(one, two):
    shape = (one.shape[0] * one.shape[1], one.shape[2])
    return jnp.concatenate([one.reshape(shape), two.reshape(shape)], axis=1)


def spread_kernel(e, h_hbm, m, eps_ref, ef_ref, hf_ref, cf_ref, h, sem):
    nx, ny, nz = m.shape
    step = nx // PARTS
    loads = []
    for i in range(PARTS):
        part = pl.ds(i * step, step)
        loads.append(pltpu.make_async_copy(h_hbm.at[:, part], h.at[:, part], sem.at[i]))
    for one in loads:
        one.start()
    values = [0.25 * eps_ref[k] for k in range(4)]
    eye = eye_like(0, nz)
    ahead = eye_like(1, nz) - eye
    none = jnp.zeros((nz, nz), F32)
    wx = square(2.0 * eye, none, ahead, eye)
    wy = square(2.0 * eye, none, -ahead, eye)
    for x in range(nx):
        kind = m[x]
        cf_ref[x] = jnp.where(
            kind < 2, jnp.where(kind == 0, values[0], values[1]), jnp.where(kind == 2, values[2], values[3])
        )
        ef_ref[2, x, pl.ds(0, ny)] = e[2, x].astype(F32)
    for i in range(PARTS):
        loads[i].wait()
        part = pl.ds(i * step, step)
        for c, other, w in ((0, 1, wx), (1, 0, wy)):
            both = dot(side(h[c, part], e[other, part]), w)
            for k in range(step):
                x = i * step + k
                line = both[k * ny : (k + 1) * ny]
                hf_ref[c, x] = line[:, :nz]
                ef_ref[other, x, pl.ds(0, ny)] = line[:, nz:]
        for k in range(step):
            x = i * step + k
            hz = h[2, x].astype(F32)
            hf_ref[2, x] = hz + hz


def field_kernel(
    ef, hf, cf, xa_ref, xb_ref, ya_ref, yb_ref, y0_ref,
    ne_hbm, nh_hbm, fix_ref, tile_ref,
    ne, nh, gf, bz, high, beyond, esem, osem,
):
    gx, gy = lax.axis_index("gx"), lax.axis_index("gy")
    nx, ny, nz = cf.shape
    parts = esem.shape[0]
    step = nx // parts
    stores = []
    for i in range(parts):
        part = pl.ds(i * step, step)
        stores.append((
            pltpu.make_async_copy(nh.at[:, part], nh_hbm.at[:, part], osem.at[i]),
            pltpu.make_async_copy(ne.at[:, part], ne_hbm.at[:, part], esem.at[i]),
        ))

    even_x, even_y = gx % 2 == 0, gy % 2 == 0
    rows, kept = pl.ds(0, ny), pl.ds(8, ny)

    def up_z(v):
        return jnp.where(iota(v.shape, 1) == nz - 1, 0.0, pltpu.roll(v, nz - 1, 1))

    def up_row(v, edge):
        n = v.shape[0]
        return jnp.where(iota(v.shape, 0) == n - 1, edge, pltpu.roll(v, n - 1, 0))

    def either(flag, a, b):
        return jnp.where(flag, a.astype(F32), b.astype(F32))

    def rounded(v):
        return v.astype(BF16).astype(F32)

    ex, ey, ez, hx, hz = [
        either(even_y, yb_ref[pl.ds(c * nx, nx)], ya_ref[pl.ds(c * nx, nx)]) for c in range(5)
    ]
    inside = jnp.where(gy > 0, 1.0, 0.0)
    low_x = rounded(inside * (2.0 * hx - ((y0_ref[1] - ez) - (up_z(ey) - ey))))
    low_z = rounded(inside * (2.0 * hz - ((up_row(ey, 0.0) - ey) - (y0_ref[0] - ex))))
    high[0] = either(even_y, ya_ref[pl.ds(0, nx)], yb_ref[pl.ds(0, nx)])
    high[1] = either(even_y, ya_ref[pl.ds(nx, nx)], yb_ref[pl.ds(nx, nx)])
    for x in range(nx):
        gf[0, x + 1, pl.ds(7, 1)] = low_x[x : x + 1]
        gf[2, x + 1, pl.ds(7, 1)] = low_z[x : x + 1]
    far = slice(nx - 1, nx)
    fix_ref[0:1] = 2.0 * hz[far]
    fix_ref[1:2] = ey[far]
    fix_ref[2:3] = y0_ref[0, pl.ds(nx - 1, 1)] - ex[far]
    for c in range(2):
        beyond[c] = either(even_x, xa_ref[c], xb_ref[c])
    ex, ey, ez, hy, hz = [either(even_x, xb_ref[c], xa_ref[c]) for c in range(5)]
    inside = jnp.where(gx > 0, 1.0, 0.0)
    gf[1, 0, kept] = rounded(inside * (2.0 * hy - ((up_z(ex) - ex) - (ef[2, 0, rows] - ez))))
    gf[2, 0, kept] = rounded(inside * (2.0 * hz - ((ef[1, 0, rows] - ey) - (up_row(ex, 0.0) - ex))))

    far = slice(ny - 1, ny)
    fix_ref[8:9] = 2.0 * hz[far]
    fix_ref[9:10] = ef[1, 0, pl.ds(ny - 1, 1)] - ey[far]
    fix_ref[10:11] = ex[far]

    back = 2.0 * (eye_like(0, nz) - eye_like(-1, nz))
    none = jnp.zeros((nz, nz), F32)
    wb = square(back, none, none, back)
    seventh = iota((8, nz), 0) == 7

    def up_y(c, which, x):
        last = jnp.where(seventh, high[which, pl.ds(x, 1)], ef[c, x, pl.ds(ny - 7, 8)])
        return jnp.concatenate([ef[c, x, pl.ds(1, ny - 8)], last], axis=0)

    def first(x):
        ey, ez = ef[1, x, rows], ef[2, x, rows]
        eyn = ef[1, x + 1, rows] if x + 1 < nx else beyond[0]
        ezn = ef[2, x + 1, rows] if x + 1 < nx else beyond[1]
        fx = hf[0, x] - (up_y(2, 1, x) - ez)
        fy = hf[1, x] + (ezn - ez)
        fz = (hf[2, x] + (up_y(0, 0, x) - ef[0, x, rows])) - (eyn - ey)
        for c, v in enumerate((fx, fy, fz)):
            g = v.astype(BF16)
            nh[c, x] = g * BF16(0.5)
            gf[c, x + 1, kept] = g.astype(F32)

    def second(x):
        shifted = pl.ds(7, ny)
        gx_, gy_, gz_ = [gf[c, x + 1, kept] for c in range(3)]
        slot = pl.ds(x % (2 * step) * ny, ny)
        tx = (gz_ - gf[2, x + 1, shifted]) - bz[1, slot]
        ty = bz[0, slot] - (gz_ - gf[2, x, kept])
        tz = (gy_ - gf[1, x, kept]) - (gx_ - gf[0, x + 1, shifted])
        coef = cf[x]
        if x == 0:
            lines = (gz_[ny - 1 :], bz[0, slot][ny - 1 :], ef[1, 0, pl.ds(ny - 1, 1)], coef[ny - 1 :])
            for k, line in enumerate(lines):
                fix_ref[11 + k : 12 + k] = line
        if x == nx - 1:
            lines = (gz_[:1], bz[1, slot][:1], ef[0, x, pl.ds(0, 1)], coef[:1])
            for k, line in enumerate(lines):
                fix_ref[3 + k : 4 + k] = line
        for c, t in enumerate((tx, ty, tz)):
            ne[c, x] = (ef[c, x, rows] + coef * t).astype(BF16)

    for i in range(parts + 1):
        for k in range(step):
            if i < parts:
                first(i * step + k)
        if i < parts:
            part = pl.ds(i * step, step)
            both = dot(side(nh[0, part], nh[1, part]), wb)
            slot = pl.ds(i % 2 * step * ny, step * ny)
            bz[0, slot] = both[:, :nz]
            bz[1, slot] = both[:, nz:]
        for k in range(step):
            if i > 0:
                second((i - 1) * step + k)
        if i < parts:
            stores[i][0].start()
        if i > 0:
            stores[i - 1][1].start()
    tile_ref[0] = ne[0, nx - 1, pl.ds(0, 8)].astype(F32)
    tile_ref[1] = ne[1, 0, pl.ds(ny - 8, 8)].astype(F32)
    for group in stores:
        for one in group:
            one.wait()


def place_kernel(sent_ref, fix_ref, tile_ref, _, grad_ref, ne_hbm, got_ref, tile, sem):
    gx, gy = lax.axis_index("gx"), lax.axis_index("gy")
    sx, sy = lax.axis_size("gx"), lax.axis_size("gy")
    _, nx, ny, nz = ne_hbm.shape
    got_ref[...] = sent_ref[...].astype(F32)

    def corner(there, device):
        line = got_ref[pl.ds(jnp.where(there, 4 * device + 3, 3), 1), :]
        return jnp.where(there, line, 0.0)

    def rounded(v):
        return v.astype(BF16).astype(F32)

    fix = [fix_ref[k : k + 1] for k in range(16)]
    line = corner((gx < sx - 1) & (gy > 0), (gx + 1) * sy + gy - 1)
    low = rounded(jnp.where(gy > 0, 1.0, 0.0) * (fix[0] - ((line - fix[1]) - fix[2])))
    first = fix[5] + fix[6] * ((fix[3] - low) - fix[4])
    line = corner((gx > 0) & (gy < sy - 1), (gx - 1) * sy + gy + 1)
    low = rounded(jnp.where(gx > 0, 1.0, 0.0) * (fix[8] - (fix[9] - (line - fix[10]))))
    second = fix[13] + fix[14] * (fix[12] - (fix[11] - low))
    row = iota((8, nz), 0)
    tile[0] = jnp.where(row == 0, first, tile_ref[0]).astype(BF16)
    tile[1] = jnp.where(row == 7, second, tile_ref[1]).astype(BF16)
    copies = [
        pltpu.make_async_copy(tile.at[0], ne_hbm.at[0, nx - 1, pl.ds(0, 8)], sem.at[0]),
        pltpu.make_async_copy(tile.at[1], ne_hbm.at[1, 0, pl.ds(ny - 8, 8)], sem.at[1]),
    ]
    for one in copies:
        one.start()

    upper = jnp.transpose(got_ref[pl.ds(0, 128, stride=4), :])
    lower = jnp.transpose(got_ref[pl.ds(1, 128, stride=4), :])
    spots = got_ref[pl.ds(2, 128, stride=4), :].astype(I32)
    spots = spots[:, :4] + spots[:, 4:8]
    ranks = grad_ref.shape[1]
    total = jnp.zeros((2 * DL, ranks), F32)
    for k in range(4):
        hot = jnp.where(iota((128, ranks), 1) == spots[:, k : k + 1], 1.0, 0.0).astype(BF16)
        part = slice(k * DL, (k + 1) * DL)
        both = jnp.concatenate([upper[part], lower[part]], axis=0).astype(BF16)
        total = total + dot(both, hot)
    grad_ref[...] = total[:DL] + total[DL:]
    for one in copies:
        one.wait()


def per_device(
    adjoint_e, adjoint_h, material, inv_eps, forward_design, cell_slot, tile_pillars, pillar_rank
):
    _, nx, ny, nz = adjoint_e.shape
    sx, sy = lax.axis_size("gx"), lax.axis_size("gy")
    both = ("gx", "gy")
    shape = jax.ShapeDtypeStruct

    def stay(v):
        return pltpu.with_memory_space_constraint(v, pltpu.HBM)

    ranks = pillar_rank.reshape(512, 128)
    adjoint_e, adjoint_h, material, forward_design, cell_slot, tile_pillars, ranks = map(
        stay, (adjoint_e, adjoint_h, material, forward_design, cell_slot, tile_pillars, ranks)
    )

    def params(mib):
        return pltpu.CompilerParams(vmem_limit_bytes=mib * 1024 * 1024)

    def swap(v, axis, size, low):
        pairs = []
        for i in range(low, size - 1, 2):
            pairs += [(i, i + 1), (i + 1, i)]
        return lax.ppermute(v, axis, pairs)

    send, xa, xb, ya, yb, y0, e_vm, m_vm = pl.pallas_call(
        pillar_kernel,
        out_shape=(
            shape((512, 128), BF16),
            shape((5, ny, nz), BF16), shape((5, ny, nz), BF16),
            shape((5 * nx, nz), BF16), shape((5 * nx, nz), BF16),
            shape((2, nx, nz), F32),
            shape(adjoint_e.shape, BF16), shape((nx, ny, nz), I32),
        ),
        in_specs=[HBM] * 7,
        out_specs=[VM] * 8,
        scratch_shapes=[
            pltpu.VMEM((512, 128), F32), pltpu.VMEM((3, nx, ny, nz), BF16),
            pltpu.VMEM((3, nx, 8, nz), BF16), pltpu.VMEM((3, nx, 8, nz), BF16),
            pltpu.VMEM((2, nx, 8, nz), BF16),
            pltpu.VMEM((8, 512), I32), pltpu.VMEM((64, 128), I32), pltpu.VMEM((nx, ny), I32),
            pltpu.VMEM((nx, 2 * ny), I32), pltpu.VMEM((512, 128), I32),
            pltpu.VMEM((512, 2 * nz), F32),
            pltpu.SemaphoreType.DMA((PARTS,)), pltpu.SemaphoreType.DMA((PARTS,)),
            pltpu.SemaphoreType.DMA((8,)), pltpu.SemaphoreType.DMA((3,)),
        ],
        compiler_params=params(12),
        name="pillars",
    )(adjoint_e, adjoint_h, material, forward_design, cell_slot, tile_pillars, ranks)

    got = lax.all_to_all(send.reshape(128, 4, 128), both, 0, 0, tiled=True)
    got = got.reshape(512, 128)

    ya = swap(ya, "gy", sy, 0)
    yb = swap(yb, "gy", sy, 1)
    xa = swap(xa, "gx", sx, 0)
    xb = swap(xb, "gx", sx, 1)

    ef, hf, cf = pl.pallas_call(
        spread_kernel,
        out_shape=(
            shape((3, nx, ny + 8, nz), F32), shape((3, nx, ny, nz), F32), shape((nx, ny, nz), F32)
        ),
        in_specs=[VM, HBM, VM, SM],
        out_specs=[VM] * 3,
        scratch_shapes=[pltpu.VMEM((3, nx, ny, nz), BF16), pltpu.SemaphoreType.DMA((PARTS,))],
        compiler_params=params(16),
        name="spread",
    )(e_vm, adjoint_h, m_vm, inv_eps)

    new_e, new_h, fix, tiles = pl.pallas_call(
        field_kernel,
        out_shape=(
            shape(adjoint_e.shape, BF16), shape(adjoint_e.shape, BF16),
            shape((16, nz), F32), shape((2, 8, nz), F32),
        ),
        in_specs=[VM] * 8,
        out_specs=[HBM, HBM, VM, VM],
        scratch_shapes=[
            pltpu.VMEM((3, nx, ny, nz), BF16), pltpu.VMEM((3, nx, ny, nz), BF16),
            pltpu.VMEM((3, nx + 1, ny + 8, nz), F32),
            pltpu.VMEM((2, 2 * nx // CHUNKS * ny, nz), F32),
            pltpu.VMEM((2, nx, nz), F32), pltpu.VMEM((2, ny, nz), F32),
        ] + [pltpu.SemaphoreType.DMA((CHUNKS,))] * 2,
        compiler_params=params(20),
        name="fields",
    )(ef, hf, cf, xa, xb, ya, yb, y0)

    gradient, new_e = pl.pallas_call(
        place_kernel,
        out_shape=(shape((DL, 512), F32), shape(adjoint_e.shape, BF16)),
        in_specs=[VM, VM, VM, HBM],
        out_specs=[VM, HBM],
        input_output_aliases={3: 1},
        scratch_shapes=[pltpu.VMEM((512, 128), F32), pltpu.VMEM((2, 8, nz), BF16), pltpu.SemaphoreType.DMA((2,))],
        compiler_params=params(4),
        name="place",
    )(got, fix, tiles, new_e)
    return new_e, new_h, gradient


def solution(mesh):
    return jax.shard_map(
        per_device,
        mesh=mesh,
        in_specs=(
            P(None, "gx", "gy", None),
            P(None, "gx", "gy", None),
            P("gx", "gy", None),
            P(),
            P(None, "gx", "gy", None),
            P("gx", "gy"),
            P(),
            P(),
        ),
        out_specs=(P(None, "gx", "gy", None), P(None, "gx", "gy", None), P(None, ("gx", "gy"))),
        check_vma=False,
    )
```

```python
import jax
import jax.numpy as jnp
from jax import lax
from jax.experimental import pallas as pl
from jax.experimental.pallas import tpu as pltpu
from jax.sharding import PartitionSpec as P

F32, BF16, I32 = jnp.float32, jnp.bfloat16, jnp.int32
HBM = pl.BlockSpec(memory_space=pltpu.HBM)
VM = pl.BlockSpec(memory_space=pltpu.VMEM)
SM = pl.BlockSpec(memory_space=pltpu.SMEM)
DL = 32
CHUNKS = 8
PARTS = 4


def split(v):
    hi = v.astype(BF16)
    return hi, (v - hi.astype(F32)).astype(BF16)


def iota(shape, axis):
    return lax.broadcasted_iota(I32, shape, axis)


def dot(a, b):
    return jnp.dot(a, b, preferred_element_type=F32)


def lookup(table, index):
    rows = index.shape[0]
    result = jnp.zeros(index.shape, table.dtype)
    for q in range(4):
        part = jnp.broadcast_to(table[q : q + 1], (rows, 128))
        taken = jnp.take_along_axis(part, index & 127, axis=1, mode="promise_in_bounds")
        result = jnp.where(index >> 7 == q, taken, result)
    return result


def pillar_kernel(
    e_hbm, h_hbm, m_hbm, f_hbm, slot_hbm, tiles_hbm, rank_hbm,
    sent_ref, xa_ref, xb_ref, ya_ref, yb_ref, y0_ref, e, hxy, kinds,
    send_ref, m, f, y_h, tiles, rank, slot, cells, ids, acc, sem, fsem, msem, xsem,
):
    gx, gy = lax.axis_index("gx"), lax.axis_index("gy")
    _, nx, ny, nz = e.shape
    parts = sem.shape[0]
    step = nx // parts
    copies = []
    for i in range(parts):
        part = pl.ds(i * step, step)
        copies.append((
            pltpu.make_async_copy(e_hbm.at[:, part], e.at[:, part], sem.at[i]),
            pltpu.make_async_copy(f_hbm.at[:, part], f.at[:, part], fsem.at[i]),
        ))
    extra = [
        pltpu.make_async_copy(tiles_hbm.at[gx, pl.ds(gy // 8 * 8, 8)], tiles, msem.at[0]),
        pltpu.make_async_copy(rank_hbm.at[pl.ds(gx * 64, 64)], rank, msem.at[1]),
        pltpu.make_async_copy(slot_hbm, slot, msem.at[2]),
        pltpu.make_async_copy(h_hbm.at[0, :, pl.ds(ny - 8, 8)], y_h.at[0], msem.at[3]),
        pltpu.make_async_copy(h_hbm.at[2, :, pl.ds(ny - 8, 8)], y_h.at[1], msem.at[4]),
        pltpu.make_async_copy(m_hbm, m, msem.at[5]),
        pltpu.make_async_copy(h_hbm.at[pl.ds(0, 2)], hxy, msem.at[6]),
    ]
    for one in extra[:3]:
        one.start()
    for one, two in copies[:1]:
        one.start()
        two.start()
    for one, two in copies[1:]:
        one.start()
        two.start()
    for one in extra[3:]:
        one.start()

    def faces(up_ref, down_ref):
        return [
            pltpu.make_async_copy(e_hbm.at[:, nx - 1], up_ref.at[pl.ds(0, 3)], xsem.at[0]),
            pltpu.make_async_copy(h_hbm.at[pl.ds(1, 2), nx - 1], up_ref.at[pl.ds(3, 2)], xsem.at[1]),
            pltpu.make_async_copy(e_hbm.at[pl.ds(1, 2), 0], down_ref.at[pl.ds(0, 2)], xsem.at[2]),
        ]

    @pl.when(gx % 2 == 0)
    def _():
        for one in faces(xa_ref, xb_ref):
            one.start()
        xb_ref[pl.ds(2, 3)] = jnp.zeros((3, ny, nz), BF16)

    @pl.when(gx % 2 == 1)
    def _():
        for one in faces(xb_ref, xa_ref):
            one.start()
        xa_ref[pl.ds(2, 3)] = jnp.zeros((3, ny, nz), BF16)

    ids[...] = iota(ids.shape, 0)
    lanes, rows = iota((128, 128), 1), iota((128, 128), 0)

    for one in extra[:3]:
        one.wait()
    quarter = gy // 4
    ranks = rank[pl.ds(0, 16, stride=4), :]
    for q in range(1, 4):
        ranks = jnp.where(quarter == q, rank[pl.ds(q, 16, stride=4), :], ranks)
    turned = ranks
    for q in range(1, 4):
        turned = jnp.where(gy % 4 == q, pltpu.roll(ranks, 128 - 32 * q, 1), turned)
    moved = [turned] + [pltpu.roll(turned, 32 * q, 1) for q in range(1, 4)]
    lane = iota((1, 128), 1)
    own_rank = []
    for q in range(4):
        line = moved[0][4 * q : 4 * q + 1]
        for k in range(1, 4):
            line = jnp.where(lane >> 5 == k, moved[k][4 * q + k : 4 * q + k + 1], line)
        own_rank.append(line)
    owner = [line >> 9 for line in own_rank]
    hits = [rows == line for line in owner]
    ones = [jnp.where(hit, 1.0, 0.0).astype(BF16) for hit in hits]
    counter = jnp.concatenate(
        [jnp.where(rows < lanes, 1.0, 0.0), jnp.ones((128, 128), F32)], axis=1
    ).astype(BF16)
    before = jnp.zeros((128, 128), F32)
    turn = []
    for q in range(4):
        both = dot(ones[q], counter)
        count = both[:, :128] + before
        turn.append(jnp.sum(jnp.where(hits[q], count, 0.0), axis=0, keepdims=True).astype(I32))
        before = before + both[:, 128:]
    spots = []
    for q in range(4):
        place = own_rank[q] & 511
        eight = jnp.where(iota((16, 128), 0) < 4, place & 255, place & 256)
        mine = (iota((16, 128), 0) & 3 == turn[q]) & (iota((16, 128), 0) < 8)
        spots.append(jnp.where(mine, eight, 0).astype(F32).astype(BF16))
    spots = lax.dot_general(
        jnp.concatenate(ones, axis=1), jnp.concatenate(spots, axis=1),
        (((1,), (1,)), ((), ())), preferred_element_type=F32,
    )
    send_ref[pl.ds(2, 128, stride=4), :] = jnp.concatenate([spots, jnp.zeros((128, 112), F32)], axis=1)
    target = jnp.concatenate([turn[q] * 128 + owner[q] for q in range(4)], axis=0)
    own = jnp.sum(jnp.where(iota(tiles.shape, 0) == gy % 8, tiles[...], 0), axis=0, keepdims=True)
    own = jnp.concatenate([own[:, 128 * q : 128 * (q + 1)] for q in range(4)], axis=0)
    canon = ((own >> 9) & 15) * 32 + (own & 31)
    target = lookup(target, canon)
    cells[:, :ny] = slot[...]
    cells[:, ny:] = slot[...]
    half = nx // 2
    pair = jnp.where(
        iota((half, 2 * ny), 1) < ny,
        cells[pl.ds(0, half, stride=2), :], cells[pl.ds(1, half, stride=2), :],
    )
    pair = lookup(target, pair)

    for i, (one, two) in enumerate(copies):
        one.wait()
        two.wait()
        part = pl.ds(i * step, step)
        density = e[0, part].astype(F32) * f[0, part].astype(F32)
        for c in range(1, 3):
            density = density + e[c, part].astype(F32) * f[c, part].astype(F32)
        both = jnp.concatenate(split(density.reshape(step * ny, nz)), axis=1)
        hot = jnp.concatenate(
            [
                jnp.where(ids[...] == pair[p : p + 1], 1.0, 0.0).astype(BF16)
                for p in range(i * step // 2, (i + 1) * step // 2)
            ],
            axis=1,
        )
        total = dot(hot, both)
        if i == 0:
            acc[...] = total
        elif i + 1 < parts:
            acc[...] += total
    total = acc[...] + total
    values = jnp.zeros((128, 128), F32)
    for k in range(4):
        part = total[k * 128 : (k + 1) * 128]
        hi, lo = split(part[:, :nz] + part[:, nz:])
        gather = jnp.where(lanes == 32 * k + (rows >> 2), 0.125, 0.0).astype(BF16)
        values = values + dot(hi, gather) + dot(lo, gather)
    hi, lo = split(values)
    send_ref[pl.ds(0, 128, stride=4), :] = hi.astype(F32)
    send_ref[pl.ds(1, 128, stride=4), :] = lo.astype(F32)

    for one in extra[3:5]:
        one.wait()
    tops, ends = pl.ds(0, 8), pl.ds(ny - 8, 8)
    at = iota((nx, 8 * nx), 1) - 8 * iota((nx, 8 * nx), 0)
    low = jnp.where(at == 0, 1.0, 0.0).astype(BF16)
    high = jnp.where(at == 7, 1.0, 0.0).astype(BF16)

    def face(which, one, two):
        both = jnp.concatenate([one.reshape(8 * nx, nz), two.reshape(8 * nx, nz)], axis=1)
        both = dot(which, both)
        return both[:, :nz], both[:, nz:]

    y0x, y0z = face(low, e[0, :, tops, :], e[2, :, tops, :])
    up_y = face(high, e[0, :, ends, :], e[1, :, ends, :]) + face(high, e[2, :, ends, :], y_h[0]) + face(high, y_h[1], y_h[1])[:1]
    y0_ref[0] = y0x
    y0_ref[1] = y0z

    sx, sy = lax.axis_size("gx"), lax.axis_size("gy")
    send_ref[pl.ds(3, 128, stride=4), :] = jnp.zeros((128, nz), F32)

    @pl.when((gx < sx - 1) & (gy > 0))
    def _():
        send_ref[pl.ds(4 * ((gx + 1) * sy + gy - 1) + 3, 1), :] = y0x[nx - 1 :]

    @pl.when((gx > 0) & (gy < sy - 1))
    def _():
        send_ref[pl.ds(4 * ((gx - 1) * sy + gy + 1) + 3, 1), :] = up_y[1][:1]

    sent_ref[...] = send_ref[...].astype(BF16)

    def pack(up_ref, down_ref):
        for c in range(5):
            up_ref[pl.ds(c * nx, nx)] = up_y[c].astype(BF16)
        down_ref[pl.ds(0, nx)] = y0x.astype(BF16)
        down_ref[pl.ds(nx, nx)] = y0z.astype(BF16)
        down_ref[pl.ds(2 * nx, 3 * nx)] = jnp.zeros((3 * nx, nz), BF16)

    @pl.when(gy % 2 == 0)
    def _():
        pack(ya_ref, yb_ref)

    @pl.when(gy % 2 == 1)
    def _():
        pack(yb_ref, ya_ref)

    extra[5].wait()
    for p in range(nx // 16):
        packed = m[16 * p]
        for k in range(1, 16):
            packed = packed | (m[16 * p + k] << (2 * k))
        kinds[p] = packed
    for one in extra[6:] + faces(xa_ref, xb_ref):
        one.wait()


def eye_like(distance, n):
    return jnp.where(iota((n, n), 0) == iota((n, n), 1) + distance, 1.0, 0.0)


def square(a, b, c, d):
    top, bottom = jnp.concatenate([a, b], axis=1), jnp.concatenate([c, d], axis=1)
    return jnp.concatenate([top, bottom], axis=0).astype(BF16)


def side(one, two):
    shape = (one.shape[0] * one.shape[1], one.shape[2])
    return jnp.concatenate([one.reshape(shape), two.reshape(shape)], axis=1)


def spread_kernel(e, hxy, kinds, h_hbm, eps_ref, ef_ref, hf_ref, cf_ref, hz, sem):
    _, nx, ny, nz = e.shape
    step = nx // PARTS
    load = pltpu.make_async_copy(h_hbm.at[2], hz, sem)
    load.start()
    values = [0.25 * eps_ref[k] for k in range(4)]
    eye = eye_like(0, nz)
    ahead = eye_like(1, nz) - eye
    none = jnp.zeros((nz, nz), F32)
    wx = square(2.0 * eye, none, ahead, eye)
    wy = square(2.0 * eye, none, -ahead, eye)
    for i in range(PARTS):
        part = pl.ds(i * step, step)
        for c, other, w in ((0, 1, wx), (1, 0, wy)):
            both = dot(side(hxy[c, part], e[other, part]), w)
            for k in range(step):
                x = i * step + k
                line = both[k * ny : (k + 1) * ny]
                hf_ref[c, x] = line[:, :nz]
                ef_ref[other, x, pl.ds(0, ny)] = line[:, nz:]
        for k in range(step):
            x = i * step + k
            kind = (kinds[x // 16] >> (2 * (x % 16))) & 3
            cf_ref[x] = jnp.where(
                kind < 2, jnp.where(kind == 0, values[0], values[1]), jnp.where(kind == 2, values[2], values[3])
            )
            ef_ref[2, x, pl.ds(0, ny)] = e[2, x].astype(F32)
    load.wait()
    for x in range(nx):
        line = hz[x].astype(F32)
        hf_ref[2, x] = line + line


def field_kernel(
    ef, hf, cf, xa_ref, xb_ref, ya_ref, yb_ref, y0_ref,
    ne_hbm, nh_hbm, fix_ref, tile_ref,
    ne, nh, gf, bz, high, beyond, esem, osem,
):
    gx, gy = lax.axis_index("gx"), lax.axis_index("gy")
    nx, ny, nz = cf.shape
    parts = esem.shape[0]
    step = nx // parts
    stores = []
    for i in range(parts):
        part = pl.ds(i * step, step)
        stores.append((
            pltpu.make_async_copy(nh.at[:, part], nh_hbm.at[:, part], osem.at[i]),
            pltpu.make_async_copy(ne.at[:, part], ne_hbm.at[:, part], esem.at[i]),
        ))

    even_x, even_y = gx % 2 == 0, gy % 2 == 0
    rows, kept = pl.ds(0, ny), pl.ds(8, ny)

    def up_z(v):
        return jnp.where(iota(v.shape, 1) == nz - 1, 0.0, pltpu.roll(v, nz - 1, 1))

    def up_row(v, edge):
        n = v.shape[0]
        return jnp.where(iota(v.shape, 0) == n - 1, edge, pltpu.roll(v, n - 1, 0))

    def either(flag, a, b):
        return jnp.where(flag, a.astype(F32), b.astype(F32))

    def rounded(v):
        return v.astype(BF16).astype(F32)

    ex, ey, ez, hx, hz = [
        either(even_y, yb_ref[pl.ds(c * nx, nx)], ya_ref[pl.ds(c * nx, nx)]) for c in range(5)
    ]
    inside = jnp.where(gy > 0, 1.0, 0.0)
    low_x = rounded(inside * (2.0 * hx - ((y0_ref[1] - ez) - (up_z(ey) - ey))))
    low_z = rounded(inside * (2.0 * hz - ((up_row(ey, 0.0) - ey) - (y0_ref[0] - ex))))
    high[0] = either(even_y, ya_ref[pl.ds(0, nx)], yb_ref[pl.ds(0, nx)])
    high[1] = either(even_y, ya_ref[pl.ds(nx, nx)], yb_ref[pl.ds(nx, nx)])
    for x in range(nx):
        gf[0, x + 1, pl.ds(7, 1)] = low_x[x : x + 1]
        gf[2, x + 1, pl.ds(7, 1)] = low_z[x : x + 1]
    far = slice(nx - 1, nx)
    fix_ref[0:1] = 2.0 * hz[far]
    fix_ref[1:2] = ey[far]
    fix_ref[2:3] = y0_ref[0, pl.ds(nx - 1, 1)] - ex[far]
    for c in range(2):
        beyond[c] = either(even_x, xa_ref[c], xb_ref[c])
    ex, ey, ez, hy, hz = [either(even_x, xb_ref[c], xa_ref[c]) for c in range(5)]
    inside = jnp.where(gx > 0, 1.0, 0.0)
    gf[1, 0, kept] = rounded(inside * (2.0 * hy - ((up_z(ex) - ex) - (ef[2, 0, rows] - ez))))
    gf[2, 0, kept] = rounded(inside * (2.0 * hz - ((ef[1, 0, rows] - ey) - (up_row(ex, 0.0) - ex))))

    far = slice(ny - 1, ny)
    fix_ref[8:9] = 2.0 * hz[far]
    fix_ref[9:10] = ef[1, 0, pl.ds(ny - 1, 1)] - ey[far]
    fix_ref[10:11] = ex[far]

    back = 2.0 * (eye_like(0, nz) - eye_like(-1, nz))
    none = jnp.zeros((nz, nz), F32)
    wb = square(back, none, none, back)
    seventh = iota((8, nz), 0) == 7

    def up_y(c, which, x):
        last = jnp.where(seventh, high[which, pl.ds(x, 1)], ef[c, x, pl.ds(ny - 7, 8)])
        return jnp.concatenate([ef[c, x, pl.ds(1, ny - 8)], last], axis=0)

    def first(x):
        ey, ez = ef[1, x, rows], ef[2, x, rows]
        eyn = ef[1, x + 1, rows] if x + 1 < nx else beyond[0]
        ezn = ef[2, x + 1, rows] if x + 1 < nx else beyond[1]
        fx = hf[0, x] - (up_y(2, 1, x) - ez)
        fy = hf[1, x] + (ezn - ez)
        fz = (hf[2, x] + (up_y(0, 0, x) - ef[0, x, rows])) - (eyn - ey)
        for c, v in enumerate((fx, fy, fz)):
            g = v.astype(BF16)
            nh[c, x] = g * BF16(0.5)
            gf[c, x + 1, kept] = g.astype(F32)

    def second(x):
        shifted = pl.ds(7, ny)
        gx_, gy_, gz_ = [gf[c, x + 1, kept] for c in range(3)]
        slot = pl.ds(x % (2 * step) * ny, ny)
        tx = (gz_ - gf[2, x + 1, shifted]) - bz[1, slot]
        ty = bz[0, slot] - (gz_ - gf[2, x, kept])
        tz = (gy_ - gf[1, x, kept]) - (gx_ - gf[0, x + 1, shifted])
        coef = cf[x]
        if x == 0:
            lines = (gz_[ny - 1 :], bz[0, slot][ny - 1 :], ef[1, 0, pl.ds(ny - 1, 1)], coef[ny - 1 :])
            for k, line in enumerate(lines):
                fix_ref[11 + k : 12 + k] = line
        if x == nx - 1:
            lines = (gz_[:1], bz[1, slot][:1], ef[0, x, pl.ds(0, 1)], coef[:1])
            for k, line in enumerate(lines):
                fix_ref[3 + k : 4 + k] = line
        for c, t in enumerate((tx, ty, tz)):
            ne[c, x] = (ef[c, x, rows] + coef * t).astype(BF16)

    for i in range(parts + 1):
        for k in range(step):
            if i < parts:
                first(i * step + k)
        if i < parts:
            part = pl.ds(i * step, step)
            both = dot(side(nh[0, part], nh[1, part]), wb)
            slot = pl.ds(i % 2 * step * ny, step * ny)
            bz[0, slot] = both[:, :nz]
            bz[1, slot] = both[:, nz:]
        for k in range(step):
            if i > 0:
                second((i - 1) * step + k)
        if i < parts:
            stores[i][0].start()
        if i > 0:
            stores[i - 1][1].start()
    tile_ref[0] = ne[0, nx - 1, pl.ds(0, 8)].astype(F32)
    tile_ref[1] = ne[1, 0, pl.ds(ny - 8, 8)].astype(F32)
    for group in stores:
        for one in group:
            one.wait()


def place_kernel(sent_ref, fix_ref, tile_ref, _, grad_ref, ne_hbm, got_ref, tile, sem):
    gx, gy = lax.axis_index("gx"), lax.axis_index("gy")
    sx, sy = lax.axis_size("gx"), lax.axis_size("gy")
    _, nx, ny, nz = ne_hbm.shape
    got_ref[...] = sent_ref[...].astype(F32)

    def corner(there, device):
        line = got_ref[pl.ds(jnp.where(there, 4 * device + 3, 3), 1), :]
        return jnp.where(there, line, 0.0)

    def rounded(v):
        return v.astype(BF16).astype(F32)

    fix = [fix_ref[k : k + 1] for k in range(16)]
    line = corner((gx < sx - 1) & (gy > 0), (gx + 1) * sy + gy - 1)
    low = rounded(jnp.where(gy > 0, 1.0, 0.0) * (fix[0] - ((line - fix[1]) - fix[2])))
    first = fix[5] + fix[6] * ((fix[3] - low) - fix[4])
    line = corner((gx > 0) & (gy < sy - 1), (gx - 1) * sy + gy + 1)
    low = rounded(jnp.where(gx > 0, 1.0, 0.0) * (fix[8] - (fix[9] - (line - fix[10]))))
    second = fix[13] + fix[14] * (fix[12] - (fix[11] - low))
    row = iota((8, nz), 0)
    tile[0] = jnp.where(row == 0, first, tile_ref[0]).astype(BF16)
    tile[1] = jnp.where(row == 7, second, tile_ref[1]).astype(BF16)
    copies = [
        pltpu.make_async_copy(tile.at[0], ne_hbm.at[0, nx - 1, pl.ds(0, 8)], sem.at[0]),
        pltpu.make_async_copy(tile.at[1], ne_hbm.at[1, 0, pl.ds(ny - 8, 8)], sem.at[1]),
    ]
    for one in copies:
        one.start()

    values = jnp.transpose(got_ref[pl.ds(0, 128, stride=4), :] + got_ref[pl.ds(1, 128, stride=4), :])
    spots = got_ref[pl.ds(2, 128, stride=4), :].astype(I32)
    spots = spots[:, :4] + spots[:, 4:8]
    ranks = grad_ref.shape[1]
    total = jnp.zeros((2 * DL, ranks), F32)
    for k in range(4):
        hot = jnp.where(iota((128, ranks), 1) == spots[:, k : k + 1], 1.0, 0.0).astype(BF16)
        total = total + dot(jnp.concatenate(split(values[k * DL : (k + 1) * DL]), axis=0), hot)
    grad_ref[...] = total[:DL] + total[DL:]
    for one in copies:
        one.wait()


def per_device(
    adjoint_e, adjoint_h, material, inv_eps, forward_design, cell_slot, tile_pillars, pillar_rank
):
    _, nx, ny, nz = adjoint_e.shape
    sx, sy = lax.axis_size("gx"), lax.axis_size("gy")
    both = ("gx", "gy")
    shape = jax.ShapeDtypeStruct

    def stay(v):
        return pltpu.with_memory_space_constraint(v, pltpu.HBM)

    ranks = pillar_rank.reshape(512, 128)
    adjoint_e, adjoint_h, material, forward_design, cell_slot, tile_pillars, ranks = map(
        stay, (adjoint_e, adjoint_h, material, forward_design, cell_slot, tile_pillars, ranks)
    )

    def params(mib):
        return pltpu.CompilerParams(vmem_limit_bytes=mib * 1024 * 1024)

    def swap(v, axis, size, low):
        pairs = []
        for i in range(low, size - 1, 2):
            pairs += [(i, i + 1), (i + 1, i)]
        return lax.ppermute(v, axis, pairs)

    send, xa, xb, ya, yb, y0, e_vm, h_vm, kinds = pl.pallas_call(
        pillar_kernel,
        out_shape=(
            shape((512, 128), BF16),
            shape((5, ny, nz), BF16), shape((5, ny, nz), BF16),
            shape((5 * nx, nz), BF16), shape((5 * nx, nz), BF16),
            shape((2, nx, nz), F32),
            shape(adjoint_e.shape, BF16), shape((2, nx, ny, nz), BF16), shape((nx // 16, ny, nz), I32),
        ),
        in_specs=[HBM] * 7,
        out_specs=[VM] * 9,
        scratch_shapes=[
            pltpu.VMEM((512, 128), F32), pltpu.VMEM((nx, ny, nz), I32),
            pltpu.VMEM((3, nx, ny, nz), BF16),
            pltpu.VMEM((2, nx, 8, nz), BF16),
            pltpu.VMEM((8, 512), I32), pltpu.VMEM((64, 128), I32), pltpu.VMEM((nx, ny), I32),
            pltpu.VMEM((nx, 2 * ny), I32), pltpu.VMEM((512, 128), I32),
            pltpu.VMEM((512, 2 * nz), F32),
            pltpu.SemaphoreType.DMA((PARTS,)), pltpu.SemaphoreType.DMA((PARTS,)),
            pltpu.SemaphoreType.DMA((7,)), pltpu.SemaphoreType.DMA((3,)),
        ],
        compiler_params=params(14),
        name="pillars",
    )(adjoint_e, adjoint_h, material, forward_design, cell_slot, tile_pillars, ranks)

    got = lax.all_to_all(send.reshape(128, 4, 128), both, 0, 0, tiled=True)
    got = got.reshape(512, 128)

    ya = swap(ya, "gy", sy, 0)
    yb = swap(yb, "gy", sy, 1)
    xa = swap(xa, "gx", sx, 0)
    xb = swap(xb, "gx", sx, 1)

    ef, hf, cf = pl.pallas_call(
        spread_kernel,
        out_shape=(
            shape((3, nx, ny + 8, nz), F32), shape((3, nx, ny, nz), F32), shape((nx, ny, nz), F32)
        ),
        in_specs=[VM, VM, VM, HBM, SM],
        out_specs=[VM] * 3,
        scratch_shapes=[pltpu.VMEM((nx, ny, nz), BF16), pltpu.SemaphoreType.DMA],
        compiler_params=params(16),
        name="spread",
    )(e_vm, h_vm, kinds, adjoint_h, inv_eps)

    new_e, new_h, fix, tiles = pl.pallas_call(
        field_kernel,
        out_shape=(
            shape(adjoint_e.shape, BF16), shape(adjoint_e.shape, BF16),
            shape((16, nz), F32), shape((2, 8, nz), F32),
        ),
        in_specs=[VM] * 8,
        out_specs=[HBM, HBM, VM, VM],
        scratch_shapes=[
            pltpu.VMEM((3, nx, ny, nz), BF16), pltpu.VMEM((3, nx, ny, nz), BF16),
            pltpu.VMEM((3, nx + 1, ny + 8, nz), F32),
            pltpu.VMEM((2, 2 * nx // CHUNKS * ny, nz), F32),
            pltpu.VMEM((2, nx, nz), F32), pltpu.VMEM((2, ny, nz), F32),
        ] + [pltpu.SemaphoreType.DMA((CHUNKS,))] * 2,
        compiler_params=params(20),
        name="fields",
    )(ef, hf, cf, xa, xb, ya, yb, y0)

    gradient, new_e = pl.pallas_call(
        place_kernel,
        out_shape=(shape((DL, 512), F32), shape(adjoint_e.shape, BF16)),
        in_specs=[VM, VM, VM, HBM],
        out_specs=[VM, HBM],
        input_output_aliases={3: 1},
        scratch_shapes=[pltpu.VMEM((512, 128), F32), pltpu.VMEM((2, 8, nz), BF16), pltpu.SemaphoreType.DMA((2,))],
        compiler_params=params(4),
        name="place",
    )(got, fix, tiles, new_e)
    return new_e, new_h, gradient


def solution(mesh):
    return jax.shard_map(
        per_device,
        mesh=mesh,
        in_specs=(
            P(None, "gx", "gy", None),
            P(None, "gx", "gy", None),
            P("gx", "gy", None),
            P(),
            P(None, "gx", "gy", None),
            P("gx", "gy"),
            P(),
            P(),
        ),
        out_specs=(P(None, "gx", "gy", None), P(None, "gx", "gy", None), P(None, ("gx", "gy"))),
        check_vma=False,
    )
```
